256 devices in a mesh: chan: 8 (over y_hi, x), win: 32 (over y_lo, z, core).
Axes of the slice: x: 4, y: 4 (y_hi: 2, y_lo: 2; y = y_hi * 2 + y_lo), z: 8, core: 2. Of those that a mesh axis runs over, the one named last changes fastest.
Arguments:
- raw: bfloat16 [128, 3200, 1024], P('win', None, 'chan'), may hold values from -6 to 6
- offsets: int32 [128], P('win'), may hold values from 0 to 128
- quality: int32 [128, 1024], P('win', 'chan'), may hold values 0 or 1
Outputs:
- stack: bfloat16 [384, 2, 1024, 1024], P('win', None, 'chan')
The draws below stay inside these ranges and needn't reach their ends.
All inputs are finite; a program needn't handle non-finite values. No bound on the sum of `quality` on one device may be relied on, other than what follows from the above.
Results may differ from the reference program's by a relative error of at most 0.0064.
Values may be sent and summed in bfloat16 or wider, within the bound.
A program may use at most 64 MiB of HBM per device.

```python
import math
import jax
import jax.numpy as jnp
from jax import lax

C = 1024
F = 384
L = 3072
FIRST_BIN = 60
SHIFT = 128
WINDOWS = 128
SEG = 3200


def with_ends(drawn, rng, low, largest):
    spot = [jax.random.randint(jax.random.fold_in(rng, axis), (), 0, length) for axis, length in enumerate(drawn.shape)]
    main_axis = drawn.shape.index(max(drawn.shape))
    next_to = spot[:main_axis] + [(spot[main_axis] + 1) % drawn.shape[main_axis]] + spot[main_axis + 1:]
    return drawn.at[tuple(spot)].set(low).at[tuple(next_to)].set(largest)


def levels(key, dims, cuts, least, largest):
    loudness, own = 1.0, jax.random.fold_in(key, 6)
    for axis_at, shards_of in cuts:
        heights = jnp.exp(jax.random.uniform(jax.random.fold_in(own, axis_at), (shards_of,), jnp.float32, least / len(cuts), largest / len(cuts)))
        loudness = loudness * jnp.repeat(heights, dims[axis_at] // shards_of).reshape([-1 if axis == axis_at else 1 for axis in range(len(dims))])
    return loudness


def scatter_about(stream_key, shape, spread, limit, cuts=(), kind=jnp.bfloat16):
    loudness = levels(stream_key, shape, cuts, -0.22, 0.18) if cuts else 1.0
    values = jax.random.normal(stream_key, shape, jnp.float32) * spread * loudness
    return jnp.minimum(jnp.maximum(values, -limit), limit).astype(kind)


def setup_inputs(seed: int = 0) -> dict:
    arg_keys = jax.random.split(jax.random.key(seed), 4)
    raw = scatter_about(arg_keys[0], (WINDOWS, SEG, C), 1.0, 6.0, ((0, 32), (2, 8)))
    offsets = with_ends(jax.random.randint(arg_keys[1], (WINDOWS,), 0, SHIFT + 1), jax.random.fold_in(arg_keys[1], 1), 0, SHIFT).astype(jnp.int32)
    quality = with_ends((jax.random.randint(arg_keys[2], (WINDOWS, C), 0, 8) < 7).astype(jnp.int32), jax.random.fold_in(arg_keys[2], 1), 0, 1)
    return {"raw": raw, "offsets": offsets, "quality": quality}


epsilon = 1e-05

def dft_table():
    sample_idx = jnp.arange(L, dtype=jnp.int32)
    bin_idx = FIRST_BIN + jnp.arange(F, dtype=jnp.int32)
    residue = bin_idx[:, None] * sample_idx[None, :] % L
    angles = residue.astype(jnp.float32) * (2.0 * math.pi / L)
    return jnp.concatenate([jnp.cos(angles), -jnp.sin(angles)], 0).astype(jnp.bfloat16)

def reference(raw, offsets, quality):
    table = dft_table().astype(jnp.float32)

    def transform_window(record):
        segment, shift_at, usable = record
        samples = lax.dynamic_slice_in_dim(segment, shift_at.astype(jnp.int32), L, 0).astype(jnp.float32)
        transform = jnp.dot(table, samples, preferred_element_type=jnp.float32, precision=lax.Precision.HIGHEST)
        band_power = lax.optimization_barrier(jnp.sum(transform * transform, axis=0)) / F
        whiten = lax.rsqrt(band_power + epsilon) * usable.astype(jnp.float32)
        return (transform * whiten[None, :]).reshape(2, F, C).astype(jnp.bfloat16)
    spectra = lax.map(transform_window, (raw, offsets, quality))
    by_bin = jnp.moveaxis(spectra, 2, 0)
    stack_scale = 1.0 / math.sqrt(WINDOWS)

    def bin_stack(values):
        real_in = values[:, 0, :].astype(jnp.float32)
        imag_in = values[:, 1, :].astype(jnp.float32)
        high = lax.Precision.HIGHEST
        real_part = jnp.dot(real_in.T, real_in, precision=high) + jnp.dot(imag_in.T, imag_in, precision=high)
        imag_part = jnp.dot(imag_in.T, real_in, precision=high) - jnp.dot(real_in.T, imag_in, precision=high)
        return (jnp.stack([real_part, imag_part], 0) * stack_scale).astype(jnp.bfloat16)
    return lax.map(bin_stack, by_bin)
```

```python
import math

import jax
import jax.numpy as jnp
from jax import lax
from jax.sharding import PartitionSpec as P

F = 384
L = 3072
FIRST_BIN = 60


epsilon = 1e-05


def dft_table():
    sample_idx = jnp.arange(L, dtype=jnp.int32)
    bin_idx = FIRST_BIN + jnp.arange(F, dtype=jnp.int32)
    residue = bin_idx[:, None] * sample_idx[None, :] % L
    angles = residue.astype(jnp.float32) * (2.0 * math.pi / L)
    return jnp.concatenate([jnp.cos(angles), -jnp.sin(angles)], 0).astype(jnp.bfloat16)


def cross_spectra(mine, partner):
    stack_scale = 1.0 / math.sqrt(mine.shape[0])
    real_mine = mine[:, 0]
    imag_mine = mine[:, 1]
    real_other = partner[:, 0]
    imag_other = partner[:, 1]
    real_part = jnp.einsum(
        "wfi,wfj->fij", real_mine, real_other, preferred_element_type=jnp.float32
    )
    real_part = real_part + jnp.einsum(
        "wfi,wfj->fij", imag_mine, imag_other, preferred_element_type=jnp.float32
    )
    imag_part = jnp.einsum(
        "wfi,wfj->fij", imag_mine, real_other, preferred_element_type=jnp.float32
    )
    imag_part = imag_part - jnp.einsum(
        "wfi,wfj->fij", real_mine, imag_other, preferred_element_type=jnp.float32
    )
    return (jnp.stack([real_part, imag_part], 1) * stack_scale).astype(jnp.bfloat16)


def local(raw, offsets, quality):
    table = dft_table()

    def cut_window(segment, shift_at):
        return lax.dynamic_slice_in_dim(segment, shift_at, L, 0)

    windows = jax.vmap(cut_window)(raw, offsets)
    transform = jnp.einsum("kl,wlc->wkc", table, windows, preferred_element_type=jnp.float32)
    band_power = jnp.sum(transform * transform, axis=1, keepdims=True) / F
    whiten = lax.rsqrt(band_power + epsilon) * quality.astype(jnp.float32)[:, None, :]
    block_width = raw.shape[2]
    spectra = (transform * whiten).astype(jnp.bfloat16).reshape(raw.shape[0], 2, F, block_width)
    mine = lax.all_to_all(spectra, "win", split_axis=2, concat_axis=0, tiled=True)
    by_bin = lax.all_gather(mine, "chan", axis=3, tiled=True)
    return cross_spectra(mine, by_bin)


def solution(mesh):
    in_specs = (P("win", None, "chan"), P("win"), P("win", "chan"))
    out_specs = P("win", None, "chan", None)
    return jax.shard_map(local, mesh=mesh, in_specs=in_specs, out_specs=out_specs, check_vma=False)
```

```python
import math

import jax
import jax.numpy as jnp
import numpy as np
from jax import lax
from jax.experimental import pallas as pl
from jax.experimental.pallas import tpu as pltpu
from jax.sharding import PartitionSpec as P

C = 1024
F = 384
L = 3072
FIRST_BIN = 60
WINDOWS = 128
SEG = 3200
EPSILON = 1e-05

LANES = 128
LOCAL_W = 4
BINS = 12
X_SIZE, Y_SIZE, Z_SIZE = 4, 4, 8
COLUMN = 2 * Z_SIZE
CHAN, WIN = 8, 32
GROUPS = 6
GROUP_BINS = BINS // GROUPS
MESH = pl.DeviceIdType.MESH


def table_seeds():
    bins = FIRST_BIN + np.arange(F, dtype=np.int64)
    first = 2.0 * math.pi / L * (bins[:, None] * np.arange(LANES)[None, :] % L)
    turn = 2.0 * math.pi / L * (bins * LANES % L)
    turn = np.broadcast_to(turn[:, None], (F, LANES))
    return [a.astype(np.float32) for a in (np.cos(first), -np.sin(first), np.cos(turn), -np.sin(turn))]


def spectra_kernel(off_ref, quality_ref, cos_ref, msin_ref, tcos_ref, tmsin_ref, raw_ref, out_ref,
                   table, rows, wide, pair, product, mixed, sem):
    copies = [pltpu.make_async_copy(raw_ref.at[w], rows.at[w], sem.at[w]) for w in range(LOCAL_W)]
    for copy in copies:
        copy.start()

    step = 48

    def table_rows(i, carry):
        at = pl.multiple_of(i * step, 16)
        here = pl.ds(at, step)
        below = pl.ds(pl.multiple_of(F + at, 16), step)
        c, m = cos_ref[here, :], msin_ref[here, :]
        tc, tm = tcos_ref[here, :], tmsin_ref[here, :]
        for a in range(L // LANES):
            table[here, a * LANES:(a + 1) * LANES] = c.astype(jnp.bfloat16)
            table[below, a * LANES:(a + 1) * LANES] = m.astype(jnp.bfloat16)
            c, m = c * tc - m * tm, m * tc + c * tm
        return carry

    lax.fori_loop(0, F // step, table_rows, 0)

    for first in range(0, LOCAL_W, 2):
        for half in range(2):
            w = first + half
            copies[w].wait()
            wide[...] = rows[w].astype(jnp.float32)
            pair[:, half * LANES:(half + 1) * LANES] = wide[pl.ds(off_ref[w], L), :].astype(jnp.bfloat16)
        product[...] = jnp.dot(table[...], pair[...], preferred_element_type=jnp.float32)
        power = jnp.sum(product[...] * product[...], axis=0, keepdims=True) / F
        whiten = lax.rsqrt(power + EPSILON)
        for half in range(2):
            w = first + half
            lanes = slice(half * LANES, (half + 1) * LANES)
            gain = whiten[:, lanes] * quality_ref[w:w + 1, :].astype(jnp.float32)
            for p in range(2):
                mixed[pl.ds(p * LOCAL_W + w, F, stride=8), :] = product[p * F:(p + 1) * F, lanes] * gain
    out_ref[...] = mixed[...].astype(jnp.bfloat16)


def whitened_spectra(raw, offsets, quality):
    vmem = pl.BlockSpec(memory_space=pltpu.VMEM)
    return pl.pallas_call(
        spectra_kernel,
        out_shape=jax.ShapeDtypeStruct((F * 8, LANES), jnp.bfloat16),
        in_specs=[pl.BlockSpec(memory_space=pltpu.SMEM)] + [vmem] * 5 + [pl.BlockSpec(memory_space=pl.ANY)],
        out_specs=vmem,
        scratch_shapes=[
            pltpu.VMEM((2 * F, L), jnp.bfloat16),
            pltpu.VMEM((LOCAL_W, SEG, LANES), jnp.bfloat16),
            pltpu.VMEM((SEG, LANES), jnp.float32),
            pltpu.VMEM((L, 2 * LANES), jnp.bfloat16),
            pltpu.VMEM((2 * F, 2 * LANES), jnp.float32),
            pltpu.VMEM((F * 8, LANES), jnp.float32),
            pltpu.SemaphoreType.DMA((LOCAL_W,)),
        ],
        compiler_params=pltpu.CompilerParams(vmem_limit_bytes=40 << 20),
        name="spectra",
    )(offsets, quality, *[jnp.asarray(a) for a in table_seeds()], raw)


def gather_kernel(s_ref, r_ref, t_ref, z_send, y_send, x_send, z_recv, y_recv, x_recv):
    chan, win = lax.axis_index("chan"), lax.axis_index("win")
    y_hi, x = chan // X_SIZE, chan % X_SIZE
    y_lo, spot = win // COLUMN, win % COLUMN
    y = y_hi * 2 + y_lo

    def column(i):
        return chan, y_lo * COLUMN + i

    def at_y(step):
        other = (y + step) % Y_SIZE
        return (other // 2) * X_SIZE + x, (other % 2) * COLUMN + spot

    def at_x(step):
        return y_hi * X_SIZE + (x + step) % X_SIZE, win

    def other_spot(d):
        return (spot + d) % COLUMN

    order = [d for k in range(1, COLUMN // 2) for d in (k, COLUMN - k)] + [COLUMN // 2]
    peers = [column(other_spot(d)) for d in order] + [at_y(1), at_y(3), at_y(2), at_x(1), at_x(3)]
    barrier = pltpu.get_barrier_semaphore()
    for peer in peers:
        pl.semaphore_signal(barrier, inc=1, device_id=peer, device_id_type=MESH)
    pl.semaphore_wait(barrier, len(peers))

    def remote(src, dst, send, recv, peer):
        return pltpu.make_async_remote_copy(
            src_ref=src, dst_ref=dst, send_sem=send, recv_sem=recv, device_id=peer, device_id_type=MESH)

    def bins_of(g):
        return pl.ds(g * GROUP_BINS, GROUP_BINS)

    def z_start(g, carry):
        bins = bins_of(g)
        mine, theirs = r_ref.at[y_hi, x, bins, win], t_ref.at[bins, spot]
        pltpu.make_async_copy(s_ref.at[win, bins], mine, z_recv.at[0, g]).start()
        pltpu.make_async_copy(s_ref.at[(1 - y_lo) * COLUMN + spot, bins], theirs, z_recv.at[1, g]).start()
        for d in order:
            i = other_spot(d)
            remote(s_ref.at[(1 - y_lo) * COLUMN + i, bins], theirs, z_send, z_recv.at[1, g], column(i)).start()
            remote(s_ref.at[y_lo * COLUMN + i, bins], mine, z_send, z_recv.at[0, g], column(i)).start()
        return carry

    lax.fori_loop(0, GROUPS, z_start, 0)

    def whole(ref, sem):
        pltpu.make_async_copy(ref, ref, sem).wait()

    def half(chan_y, chan_x, bins, lo):
        return r_ref.at[chan_y, chan_x, bins, pl.ds(lo * COLUMN, COLUMN)]

    for t in range(GROUPS + 2):
        if t < GROUPS:
            bins = bins_of(t)
            mine = half(y_hi, x, bins, y_lo)
            whole(t_ref.at[bins], z_recv.at[1, t])
            remote(t_ref.at[bins], mine, y_send.at[0], y_recv.at[0, t], at_y(1)).start()
            remote(t_ref.at[bins], mine, y_send.at[1], y_recv.at[1, t], at_y(3)).start()
            whole(mine, z_recv.at[0, t])
            remote(mine, mine, y_send.at[2], y_recv.at[2, t], at_y(2)).start()
        if 0 <= t - 1 < GROUPS:
            g = t - 1
            bins = bins_of(g)
            for k, step in ((0, 3), (1, 1), (2, 2)):
                other = (y + step) % Y_SIZE
                whole(half(other // 2, x, bins, other % 2), y_recv.at[k, g])
            block = r_ref.at[:, x, bins]
            remote(block, block, x_send.at[0], x_recv.at[0, g], at_x(1)).start()
            remote(block, block, x_send.at[1], x_recv.at[1, g], at_x(3)).start()
        if 0 <= t - 2 < GROUPS:
            g = t - 2
            bins = bins_of(g)
            left, right = (x + 3) % X_SIZE, (x + 1) % X_SIZE
            whole(r_ref.at[:, left, bins], x_recv.at[0, g])
            block = r_ref.at[0, left, bins]
            remote(block, block, x_send.at[2], x_recv.at[2, g], at_x(1)).start()
            whole(r_ref.at[:, right, bins], x_recv.at[1, g])
            block = r_ref.at[1, right, bins]
            remote(block, block, x_send.at[3], x_recv.at[3, g], at_x(3)).start()

    far = (x + 2) % X_SIZE
    for g in range(GROUPS):
        for k in range(2):
            whole(r_ref.at[k, far, bins_of(g)], x_recv.at[2 + k, g])
    whole(s_ref.at[pl.ds(0, WIN - 2)], z_send)
    for k in range(2):
        whole(t_ref, y_send.at[k])
        whole(r_ref.at[:, 0], x_send.at[k])
        whole(r_ref.at[0, 0], x_send.at[2 + k])
    whole(r_ref.at[0, 0, :, pl.ds(0, COLUMN)], y_send.at[2])


def gathered_spectra(s):
    return pl.pallas_call(
        gather_kernel,
        out_shape=jax.ShapeDtypeStruct((2, X_SIZE, BINS, WIN, 8, LANES), jnp.bfloat16),
        in_specs=[pl.BlockSpec(memory_space=pltpu.VMEM)],
        out_specs=pl.BlockSpec(memory_space=pl.ANY),
        scratch_shapes=[
            pltpu.VMEM((BINS, COLUMN, 8, LANES), jnp.bfloat16),
            pltpu.SemaphoreType.DMA,
            pltpu.SemaphoreType.DMA((3,)),
            pltpu.SemaphoreType.DMA((4,)),
            pltpu.SemaphoreType.DMA((2, GROUPS)),
            pltpu.SemaphoreType.DMA((3, GROUPS)),
            pltpu.SemaphoreType.DMA((4, GROUPS)),
        ],
        compiler_params=pltpu.CompilerParams(collective_id=0, has_side_effects=True),
        name="gather",
    )(s)


def stack_kernel(chan_ref, r_ref, out_ref):
    own = r_ref[chan_ref[0], 0].astype(jnp.float32)
    turned = pltpu.roll(own.reshape(WIN, 8, LANES), 4, 1)
    row = lax.broadcasted_iota(jnp.int32, (WIN, 8, LANES), 1)
    turned = jnp.where(row < 4, turned, -turned).reshape(WIN * 8, LANES)
    left = jnp.concatenate([own.T, turned.T], 0).astype(jnp.bfloat16)
    scale = 1.0 / math.sqrt(WINDOWS)
    for k in range(0, CHAN, 2):
        right = jnp.concatenate([r_ref[k, 0], r_ref[k + 1, 0]], 1)
        part = jnp.dot(left, right, preferred_element_type=jnp.float32) * scale
        lanes = slice(k * LANES, (k + 2) * LANES)
        out_ref[0, 0, :, lanes] = part[:LANES].astype(jnp.bfloat16)
        out_ref[0, 1, :, lanes] = part[LANES:].astype(jnp.bfloat16)


def stacked(chan, r):
    return pl.pallas_call(
        stack_kernel,
        out_shape=jax.ShapeDtypeStruct((BINS, 2, LANES, C), jnp.bfloat16),
        grid_spec=pltpu.PrefetchScalarGridSpec(
            num_scalar_prefetch=1,
            grid=(BINS,),
            in_specs=[pl.BlockSpec((CHAN, 1, WIN * 8, LANES), lambda f, _: (0, f, 0, 0))],
            out_specs=pl.BlockSpec((1, 2, LANES, C), lambda f, _: (f, 0, 0, 0)),
        ),
        name="stack",
    )(chan, r)


def local(raw, offsets, quality):
    s = whitened_spectra(raw, offsets, quality)
    r = gathered_spectra(s.reshape(WIN, BINS, 8, LANES))
    chan = lax.axis_index("chan").astype(jnp.int32).reshape(1)
    return stacked(chan, r.reshape(CHAN, BINS, WIN * 8, LANES))


def solution(mesh):
    in_specs = (P("win", None, "chan"), P("win"), P("win", "chan"))
    out_specs = P("win", None, "chan", None)
    return jax.shard_map(local, mesh=mesh, in_specs=in_specs, out_specs=out_specs, check_vma=False)
```

```python
import math

import jax
import jax.numpy as jnp
import numpy as np
from jax import lax
from jax.experimental import pallas as pl
from jax.experimental.pallas import tpu as pltpu
from jax.sharding import PartitionSpec as P

C = 1024
F = 384
L = 3072
FIRST_BIN = 60
WINDOWS = 128
SEG = 3200
EPSILON = 1e-05

LANES = 128
LOCAL_W = 4
BINS = 12
X_SIZE, Y_SIZE, Z_SIZE = 4, 4, 8
COLUMN = 2 * Z_SIZE
CHAN, WIN = 8, 32
GROUPS = (("y", 0, 1), ("x", 1, 1), ("y", 2, 2), ("x", 4, 2), ("x", 6, 2), ("y", 8, 2), ("y", 10, 1), ("y", 11, 1))
ORDER = (
    ("zy", 0), ("zx", 1), ("uy", 0), ("zy", 2), ("x2x", 1), ("yx", 0),
    ("y1", 1), ("zx", 3), ("uy", 2), ("x2y", 0), ("ux", 1), ("zx", 4),
    ("x2x", 3), ("zy", 5), ("yx", 2), ("ey", 0), ("zy", 6), ("ex", 1),
    ("zy", 7), ("x2x", 4), ("uy", 5), ("y1", 3), ("uy", 6), ("uy", 7),
    ("yx", 5), ("ux", 3), ("x2y", 2), ("y1", 4), ("yx", 6), ("yx", 7),
    ("x2y", 5), ("ex", 3), ("ey", 2), ("ux", 4), ("x2y", 6), ("x2y", 7),
    ("ey", 5), ("ex", 4), ("ey", 6), ("ey", 7),
)
MESH = pl.DeviceIdType.MESH


def table_seeds():
    bins = FIRST_BIN + np.arange(F, dtype=np.int64)
    first = 2.0 * math.pi / L * (bins[:, None] * np.arange(LANES)[None, :] % L)
    turn = 2.0 * math.pi / L * (bins * LANES % L)
    turn = np.broadcast_to(turn[:, None], (F, LANES))
    return np.stack([np.cos(first), -np.sin(first), np.cos(turn), -np.sin(turn)]).astype(np.float32)


def spectra_kernel(off_hbm, quality_hbm, seeds_hbm, raw_hbm, out_ref,
                   off_ref, quality_ref, seeds, table, rows, wide, pair, product, mixed, sem):
    seeds_copy = pltpu.make_async_copy(seeds_hbm, seeds, sem.at[LOCAL_W])
    small = [pltpu.make_async_copy(off_hbm, off_ref, sem.at[LOCAL_W + 1]),
             pltpu.make_async_copy(quality_hbm, quality_ref, sem.at[LOCAL_W + 2])]
    copies = [pltpu.make_async_copy(raw_hbm.at[w], rows.at[w], sem.at[w]) for w in range(LOCAL_W)]
    for copy in [seeds_copy] + small + copies:
        copy.start()
    seeds_copy.wait()

    step = 48

    def table_rows(i, carry):
        at = pl.multiple_of(i * step, 16)
        here = pl.ds(at, step)
        below = pl.ds(pl.multiple_of(F + at, 16), step)
        c, m = seeds[0, here, :], seeds[1, here, :]
        tc, tm = seeds[2, here, :], seeds[3, here, :]
        for a in range(L // LANES):
            table[here, a * LANES:(a + 1) * LANES] = c.astype(jnp.bfloat16)
            table[below, a * LANES:(a + 1) * LANES] = m.astype(jnp.bfloat16)
            c, m = c * tc - m * tm, m * tc + c * tm
        return carry

    lax.fori_loop(0, F // step, table_rows, 0)
    for copy in small:
        copy.wait()

    for first in range(0, LOCAL_W, 2):
        for half in range(2):
            w = first + half
            copies[w].wait()
            wide[half] = rows[w].astype(jnp.float32)
            pair[:, half * LANES:(half + 1) * LANES] = wide[half, pl.ds(off_ref[w], L), :].astype(jnp.bfloat16)
        product[...] = jnp.dot(table[...], pair[...], preferred_element_type=jnp.float32)
        power = jnp.sum(product[...] * product[...], axis=0, keepdims=True) / F
        whiten = lax.rsqrt(power + EPSILON)
        for half in range(2):
            w = first + half
            lanes = slice(half * LANES, (half + 1) * LANES)
            gain = whiten[:, lanes] * quality_ref[w:w + 1, :].astype(jnp.float32)
            for p in range(2):
                mixed[pl.ds(p * LOCAL_W + w, F, stride=8), :] = product[p * F:(p + 1) * F, lanes] * gain
    out_ref[...] = mixed[...].astype(jnp.bfloat16)


def whitened_spectra(raw, offsets, quality):
    anywhere = pl.BlockSpec(memory_space=pl.ANY)
    return pl.pallas_call(
        spectra_kernel,
        out_shape=jax.ShapeDtypeStruct((F * 8, LANES), jnp.bfloat16),
        in_specs=[anywhere] * 4,
        out_specs=pl.BlockSpec(memory_space=pltpu.VMEM),
        scratch_shapes=[
            pltpu.SMEM((LOCAL_W,), jnp.int32),
            pltpu.VMEM((LOCAL_W, LANES), jnp.int32),
            pltpu.VMEM((4, F, LANES), jnp.float32),
            pltpu.VMEM((2 * F, L), jnp.bfloat16),
            pltpu.VMEM((LOCAL_W, SEG, LANES), jnp.bfloat16),
            pltpu.VMEM((2, SEG, LANES), jnp.float32),
            pltpu.VMEM((L, 2 * LANES), jnp.bfloat16),
            pltpu.VMEM((2 * F, 2 * LANES), jnp.float32),
            pltpu.VMEM((F * 8, LANES), jnp.float32),
            pltpu.SemaphoreType.DMA((LOCAL_W + 3,)),
        ],
        compiler_params=pltpu.CompilerParams(vmem_limit_bytes=67043328),
        name="spectra",
    )(offsets, quality, jnp.asarray(table_seeds()), raw)


def gather_kernel(s_ref, r_ref, t_ref, u_ref, z_send, send_sem, z_recv, y_recv, u_recv, x_recv):
    chan, win = lax.axis_index("chan"), lax.axis_index("win")
    y_hi, x = chan // X_SIZE, chan % X_SIZE
    y_lo, spot = win // COLUMN, win % COLUMN
    y = y_hi * 2 + y_lo
    left, right, far = (x + 3) % X_SIZE, (x + 1) % X_SIZE, (x + 2) % X_SIZE

    def column(i):
        return chan, y_lo * COLUMN + i

    def at_y(step):
        other = (y + step) % Y_SIZE
        return (other // 2) * X_SIZE + x, (other % 2) * COLUMN + spot

    to_right, to_left, to_up, to_down = (y_hi * X_SIZE + right, win), (y_hi * X_SIZE + left, win), at_y(1), at_y(3)

    def other_spot(d):
        return (spot + d) % COLUMN

    order = [d for k in range(1, COLUMN // 2) for d in (k, COLUMN - k)] + [COLUMN // 2]
    peers = [column(other_spot(d)) for d in order] + [to_up, to_down, to_right, to_left]
    barrier = pltpu.get_barrier_semaphore()
    for peer in peers:
        pl.semaphore_signal(barrier, inc=1, device_id=peer, device_id_type=MESH)
    pl.semaphore_wait(barrier, len(peers))

    def remote(src, dst, send, recv, peer):
        return pltpu.make_async_remote_copy(
            src_ref=src, dst_ref=dst, send_sem=send, recv_sem=recv, device_id=peer, device_id_type=MESH)

    started = []

    def start(k, g, src, dst, recv, peer):
        copy = remote(src, dst, send_sem.at[k, g], recv, peer)
        copy.start()
        started.append(copy)

    def whole(ref, sem):
        pltpu.make_async_copy(ref, ref, sem).wait()

    spans = [pl.ds(first, count) for _, first, count in GROUPS]
    for g, bins in enumerate(spans):
        mine, theirs = r_ref.at[y_hi, x, bins, win], t_ref.at[x, bins, spot]
        pltpu.make_async_copy(s_ref.at[(1 - y_lo) * COLUMN + spot, bins], theirs, z_recv.at[0, g]).start()
        pltpu.make_async_copy(s_ref.at[win, bins], mine, z_recv.at[1, g]).start()

        def spread(d):
            i = other_spot(d)
            remote(s_ref.at[(1 - y_lo) * COLUMN + i, bins], theirs, z_send, z_recv.at[0, g], column(i)).start()
            remote(s_ref.at[y_lo * COLUMN + i, bins], mine, z_send, z_recv.at[1, g], column(i)).start()

        def both_ways(k, carry):
            spread(k)
            spread(COLUMN - k)
            return carry

        lax.fori_loop(1, COLUMN // 2, both_ways, 0)
        spread(COLUMN // 2)

    def part(chan_y, xs, bins, lo, first=0, count=COLUMN):
        return r_ref.at[chan_y, xs, bins, pl.ds(lo * COLUMN + first, count)]

    def along_y(g, bins, xs):
        mine = part(y_hi, xs, bins, y_lo)
        start(0, g, t_ref.at[xs, bins], mine, y_recv.at[0, g], to_up)
        start(1, g, t_ref.at[xs, bins], mine, y_recv.at[1, g], to_down)

    def along_y_far(g, bins, xs):
        for way, peer in ((0, to_up), (1, to_down)):
            start(2 + way, g, part(y_hi, xs, bins, y_lo, 8 * way, 8), u_ref.at[way, xs, bins], u_recv.at[way, g], peer)

    def relay_y(g, bins, xs):
        for way, peer, step in ((0, to_up, 3), (1, to_down, 1)):
            whole(u_ref.at[way, xs, bins], u_recv.at[way, g])
            other = (y + step) % Y_SIZE
            start(4 + way, g, u_ref.at[way, xs, bins], part(other // 2, xs, bins, other % 2, 8 * way, 8),
                  y_recv.at[2 + way, g], peer)

    def wait_y(g, bins, xs):
        for k, step in ((0, 3), (1, 1)):
            other = (y + step) % Y_SIZE
            whole(part(other // 2, xs, bins, other % 2), y_recv.at[k, g])
        for way in range(2):
            whole(part(1 - y_hi, xs, bins, y_lo, 8 * way, 8), y_recv.at[2 + way, g])

    def act(what, g):
        bins = spans[g]
        if what == "zy":
            whole(t_ref.at[x, bins], z_recv.at[0, g])
            along_y(g, bins, x)
            whole(part(y_hi, x, bins, y_lo), z_recv.at[1, g])
            along_y_far(g, bins, x)
        elif what == "uy":
            relay_y(g, bins, x)
        elif what == "yx":
            wait_y(g, bins, x)
            block = r_ref.at[:, x, bins]
            start(6, g, block, block, x_recv.at[0, g], to_right)
            start(7, g, block, block, x_recv.at[1, g], to_left)
        elif what == "x2y":
            whole(r_ref.at[:, left, bins], x_recv.at[0, g])
            block = r_ref.at[0, left, bins]
            start(8, g, block, block, x_recv.at[4, g], to_right)
            whole(r_ref.at[:, right, bins], x_recv.at[1, g])
            block = r_ref.at[1, right, bins]
            start(9, g, block, block, x_recv.at[5, g], to_left)
        elif what == "ey":
            for k in range(2):
                whole(r_ref.at[k, far, bins], x_recv.at[4 + k, g])
        elif what == "zx":
            block = t_ref.at[x, bins]
            whole(block, z_recv.at[0, g])
            start(6, g, block, block, x_recv.at[0, g], to_right)
            start(7, g, block, block, x_recv.at[1, g], to_left)
            block = part(y_hi, x, bins, y_lo)
            whole(block, z_recv.at[1, g])
            start(8, g, block, block, x_recv.at[2, g], to_right)
            start(9, g, block, block, x_recv.at[3, g], to_left)
        elif what == "x2x":
            block = t_ref.at[left, bins]
            whole(block, x_recv.at[0, g])
            start(10, g, block, block, x_recv.at[4, g], to_right)
            block = part(y_hi, right, bins, y_lo)
            whole(block, x_recv.at[3, g])
            start(11, g, block, block, x_recv.at[5, g], to_left)
        elif what == "y1":
            whole(t_ref.at[right, bins], x_recv.at[1, g])
            whole(part(y_hi, left, bins, y_lo), x_recv.at[2, g])
            whole(t_ref.at[far, bins], x_recv.at[4, g])
            whole(part(y_hi, far, bins, y_lo), x_recv.at[5, g])
            along_y_far(g, bins, slice(None))
            along_y(g, bins, slice(None))
        elif what == "ux":
            relay_y(g, bins, slice(None))
        elif what == "ex":
            wait_y(g, bins, slice(None))

    for what, g in ORDER:
        act(what, g)
    whole(s_ref.at[pl.ds(0, WIN - 2)], z_send)
    for copy in started:
        copy.wait_send()


def gathered_spectra(s):
    n = len(GROUPS)
    return pl.pallas_call(
        gather_kernel,
        out_shape=jax.ShapeDtypeStruct((2, X_SIZE, BINS, WIN, 8, LANES), jnp.bfloat16),
        in_specs=[pl.BlockSpec(memory_space=pltpu.VMEM)],
        out_specs=pl.BlockSpec(memory_space=pl.ANY),
        scratch_shapes=[
            pltpu.VMEM((X_SIZE, BINS, COLUMN, 8, LANES), jnp.bfloat16),
            pltpu.VMEM((2, X_SIZE, BINS, 8, 8, LANES), jnp.bfloat16),
            pltpu.SemaphoreType.DMA,
            pltpu.SemaphoreType.DMA((12, n)),
            pltpu.SemaphoreType.DMA((2, n)),
            pltpu.SemaphoreType.DMA((4, n)),
            pltpu.SemaphoreType.DMA((2, n)),
            pltpu.SemaphoreType.DMA((6, n)),
        ],
        compiler_params=pltpu.CompilerParams(
            collective_id=0, has_side_effects=True, vmem_limit_bytes=48 << 20),
        name="gather",
    )(s)


def stack_kernel(r_hbm, out_hbm, r_ref, out_ref, r_sem, out_sem):
    reads = [pltpu.make_async_copy(r_hbm.at[:, f], r_ref.at[f], r_sem.at[f]) for f in range(BINS)]
    for read in reads:
        read.start()
    chan = lax.axis_index("chan")
    row = lax.broadcasted_iota(jnp.int32, (WIN, 8, LANES), 1)
    scale = 1.0 / math.sqrt(WINDOWS)

    def one_bin(f, carry):
        pltpu.make_async_copy(r_hbm.at[:, f], r_ref.at[f], r_sem.at[f]).wait()
        own = r_ref[f, chan].astype(jnp.float32)
        turned = pltpu.roll(own.reshape(WIN, 8, LANES), 4, 1)
        turned = jnp.where(row < 4, turned, -turned).reshape(WIN * 8, LANES)
        ours = jnp.concatenate([own.T, turned.T], 0).astype(jnp.bfloat16)
        for k in range(0, CHAN, 2):
            pair = jnp.concatenate([r_ref[f, k], r_ref[f, k + 1]], 1)
            both = jnp.dot(ours, pair, preferred_element_type=jnp.float32) * scale
            lanes = slice(k * LANES, (k + 2) * LANES)
            out_ref[f, 0, :, lanes] = both[:LANES].astype(jnp.bfloat16)
            out_ref[f, 1, :, lanes] = both[LANES:].astype(jnp.bfloat16)
        pltpu.make_async_copy(out_ref.at[f], out_hbm.at[f], out_sem.at[f]).start()
        return carry

    lax.fori_loop(0, BINS, one_bin, 0)
    for f in range(BINS):
        pltpu.make_async_copy(out_ref.at[f], out_hbm.at[f], out_sem.at[f]).wait()


def stacked(r):
    anywhere = pl.BlockSpec(memory_space=pl.ANY)
    return pl.pallas_call(
        stack_kernel,
        out_shape=jax.ShapeDtypeStruct((BINS, 2, LANES, C), jnp.bfloat16),
        in_specs=[anywhere],
        out_specs=anywhere,
        scratch_shapes=[
            pltpu.VMEM((BINS, CHAN, WIN * 8, LANES), jnp.bfloat16),
            pltpu.VMEM((BINS, 2, LANES, C), jnp.bfloat16),
            pltpu.SemaphoreType.DMA((BINS,)),
            pltpu.SemaphoreType.DMA((BINS,)),
        ],
        compiler_params=pltpu.CompilerParams(vmem_limit_bytes=67043328),
        name="stack",
    )(r)


def local(raw, offsets, quality):
    s = whitened_spectra(raw, offsets, quality)
    r = gathered_spectra(s.reshape(WIN, BINS, 8, LANES))
    return stacked(r.reshape(CHAN, BINS, WIN * 8, LANES))


def solution(mesh):
    in_specs = (P("win", None, "chan"), P("win"), P("win", "chan"))
    out_specs = P("win", None, "chan", None)
    return jax.shard_map(local, mesh=mesh, in_specs=in_specs, out_specs=out_specs, check_vma=False)
```

```python
import math

import jax
import jax.numpy as jnp
import numpy as np
from jax import lax
from jax.experimental import pallas as pl
from jax.experimental.pallas import tpu as pltpu
from jax.sharding import PartitionSpec as P

C = 1024
F = 384
L = 3072
FIRST_BIN = 60
WINDOWS = 128
SEG = 3200
EPSILON = 1e-05

LANES = 128
LOCAL_W = 4
BINS = 12
X_SIZE, Y_SIZE, Z_SIZE = 4, 4, 8
COLUMN = 2 * Z_SIZE
CHAN, WIN = 8, 32
GROUPS = (("y", 0, 1), ("x", 1, 1), ("y", 2, 2), ("x", 4, 2), ("x", 6, 2), ("y", 8, 2), ("y", 10, 1), ("y", 11, 1))
ORDER = (
    ("zy", 0), ("zx", 1), ("zy", 2), ("x2x", 1), ("yx", 0),
    ("y1", 1), ("zx", 3), ("x2y", 0), ("zx", 4),
    ("x2x", 3), ("zy", 5), ("yx", 2), ("ey", 0), ("zy", 6), ("ex", 1),
    ("zy", 7), ("x2x", 4), ("y1", 3),
    ("yx", 5), ("x2y", 2), ("y1", 4), ("yx", 6), ("yx", 7),
    ("x2y", 5), ("ex", 3), ("ey", 2), ("x2y", 6), ("x2y", 7),
    ("ey", 5), ("ex", 4), ("ey", 6), ("ey", 7),
)
MESH = pl.DeviceIdType.MESH


def table_seeds():
    bins = FIRST_BIN + np.arange(F, dtype=np.int64)
    first = 2.0 * math.pi / L * (bins[:, None] * np.arange(LANES)[None, :] % L)
    turn = 2.0 * math.pi / L * (bins * LANES % L)
    turn = np.broadcast_to(turn[:, None], (F, LANES))
    return np.stack([np.cos(first), -np.sin(first), np.cos(turn), -np.sin(turn)]).astype(np.float32)


def spectra_kernel(off_hbm, quality_hbm, seeds_hbm, raw_hbm, s_ref,
                   off_ref, quality_ref, seeds, table, rows, wide, pairs, product, mixed, sem):
    seeds_copy = pltpu.make_async_copy(seeds_hbm, seeds, sem.at[LOCAL_W])
    small = [pltpu.make_async_copy(off_hbm, off_ref, sem.at[LOCAL_W + 1]),
             pltpu.make_async_copy(quality_hbm, quality_ref, sem.at[LOCAL_W + 2])]
    copies = [pltpu.make_async_copy(raw_hbm.at[w], rows.at[w], sem.at[w]) for w in range(LOCAL_W)]
    for copy in [seeds_copy] + small + copies[:1]:
        copy.start()
    seeds_copy.wait()
    for copy in copies[1:]:
        copy.start()

    step, half_blocks = 48, L // LANES // 2
    row = lax.broadcasted_iota(jnp.int32, (step, LANES), 0)
    sign = jnp.where(row % 2 == FIRST_BIN % 2, 1.0, -1.0).astype(jnp.bfloat16)

    def table_rows(i, carry):
        at = pl.multiple_of(i * step, 16)
        c, m = seeds[0, pl.ds(at, step), :], seeds[1, pl.ds(at, step), :]
        tc, tm = seeds[2, pl.ds(at, step), :], seeds[3, pl.ds(at, step), :]
        for a in range(half_blocks):
            for v, first in ((c, at), (m, pl.multiple_of(F + at, 16))):
                v = v.astype(jnp.bfloat16)
                here = pl.ds(first, step)
                table[here, a * LANES:(a + 1) * LANES] = v
                table[here, (a + half_blocks) * LANES:(a + half_blocks + 1) * LANES] = v * sign
            c, m = c * tc - m * tm, m * tc + c * tm
        return carry

    lax.fori_loop(0, F // step, table_rows, 0)
    for copy in small:
        copy.wait()

    def cut(w, lo, hi):
        if lo == 0:
            copies[w].wait()
            wide[w % 2] = rows[w].astype(jnp.float32)
        lanes = slice(w % 2 * LANES, (w % 2 + 1) * LANES)
        pairs[w // 2, lo:hi, lanes] = wide[w % 2, pl.ds(off_ref[w] + lo, hi - lo), :].astype(jnp.bfloat16)

    cut(0, 0, L)
    cut(1, 0, L)
    for first in range(0, LOCAL_W, 2):
        chunk, tile = L // 3, 2 * F // 6
        for i in range(6):
            at = slice(i * tile, (i + 1) * tile)
            product[at] = jnp.dot(table[at], pairs[first // 2], preferred_element_type=jnp.float32)
            if first + 2 < LOCAL_W:
                cut(first + 2 + i // 3, i % 3 * chunk, (i % 3 + 1) * chunk)
        power = jnp.sum(product[...] * product[...], axis=0, keepdims=True) / F
        whiten = lax.rsqrt(power + EPSILON)
        for half in range(2):
            w = first + half
            lanes = slice(half * LANES, (half + 1) * LANES)
            gain = whiten[:, lanes] * quality_ref[w:w + 1, :].astype(jnp.float32)
            for p in range(2):
                mixed[pl.ds(p * LOCAL_W + w, F, stride=8), :] = product[p * F:(p + 1) * F, lanes] * gain
    s_ref[...] = mixed[...].astype(jnp.bfloat16).reshape(WIN, BINS, 8, LANES)


def gather_kernel(off_hbm, quality_hbm, seeds_hbm, raw_hbm, r_ref,
                  s_ref, t_ref, z_send, send_sem, z_recv, y_recv, x_recv, *spectra_scratch):
    def spectra():
        spectra_kernel(off_hbm, quality_hbm, seeds_hbm, raw_hbm, s_ref, *spectra_scratch)

    chan, win = lax.axis_index("chan"), lax.axis_index("win")
    y_hi, x = chan // X_SIZE, chan % X_SIZE
    y_lo, spot = win // COLUMN, win % COLUMN
    y = y_hi * 2 + y_lo
    left, right, far = (x + 3) % X_SIZE, (x + 1) % X_SIZE, (x + 2) % X_SIZE

    def column(i):
        return chan, y_lo * COLUMN + i

    def at_y(step):
        other = (y + step) % Y_SIZE
        return (other // 2) * X_SIZE + x, (other % 2) * COLUMN + spot

    to_right, to_left, to_up, to_down = (y_hi * X_SIZE + right, win), (y_hi * X_SIZE + left, win), at_y(1), at_y(3)

    def other_spot(d):
        return (spot + d) % COLUMN

    order = [d for k in range(1, COLUMN // 2) for d in (k, COLUMN - k)] + [COLUMN // 2]
    peers = [column(other_spot(d)) for d in order] + [to_up, to_down, at_y(2), to_right, to_left]
    barrier = pltpu.get_barrier_semaphore()
    for peer in peers:
        pl.semaphore_signal(barrier, inc=1, device_id=peer, device_id_type=MESH)

    spectra()
    pl.semaphore_wait(barrier, len(peers))

    def remote(src, dst, send, recv, peer):
        return pltpu.make_async_remote_copy(
            src_ref=src, dst_ref=dst, send_sem=send, recv_sem=recv, device_id=peer, device_id_type=MESH)

    started = []

    def start(k, g, src, dst, recv, peer):
        copy = remote(src, dst, send_sem.at[k, g], recv, peer)
        copy.start()
        started.append(copy)

    def whole(ref, sem):
        pltpu.make_async_copy(ref, ref, sem).wait()

    spans = [pl.ds(first, count) for _, first, count in GROUPS]
    for g, bins in enumerate(spans):
        mine, theirs = r_ref.at[y_hi, x, bins, win], t_ref.at[x, bins, spot]
        pltpu.make_async_copy(s_ref.at[(1 - y_lo) * COLUMN + spot, bins], theirs, z_recv.at[0, g]).start()
        pltpu.make_async_copy(s_ref.at[win, bins], mine, z_recv.at[1, g]).start()

        def spread(d):
            i = other_spot(d)
            remote(s_ref.at[(1 - y_lo) * COLUMN + i, bins], theirs, z_send, z_recv.at[0, g], column(i)).start()
            remote(s_ref.at[y_lo * COLUMN + i, bins], mine, z_send, z_recv.at[1, g], column(i)).start()

        def both_ways(k, carry):
            spread(k)
            spread(COLUMN - k)
            return carry

        lax.fori_loop(1, COLUMN // 2, both_ways, 0)
        spread(COLUMN // 2)

    def part(chan_y, xs, bins, lo, first=0, count=COLUMN):
        return r_ref.at[chan_y, xs, bins, pl.ds(lo * COLUMN + first, count)]

    def along_y(g, bins, xs):
        mine = part(y_hi, xs, bins, y_lo)
        start(0, g, t_ref.at[xs, bins], mine, y_recv.at[0, g], to_up)
        start(1, g, t_ref.at[xs, bins], mine, y_recv.at[1, g], to_down)

    def along_y_far(g, bins, xs):
        block = part(y_hi, xs, bins, y_lo)
        start(2, g, block, block, y_recv.at[2, g], at_y(2))

    def wait_y(g, bins, xs):
        for k, step in ((0, 3), (1, 1)):
            other = (y + step) % Y_SIZE
            whole(part(other // 2, xs, bins, other % 2), y_recv.at[k, g])
        whole(part(1 - y_hi, xs, bins, y_lo), y_recv.at[2, g])

    def act(what, g):
        bins = spans[g]
        if what == "zy":
            whole(t_ref.at[x, bins], z_recv.at[0, g])
            along_y(g, bins, x)
            whole(part(y_hi, x, bins, y_lo), z_recv.at[1, g])
            along_y_far(g, bins, x)
        elif what == "yx":
            wait_y(g, bins, x)
            block = r_ref.at[:, x, bins]
            start(6, g, block, block, x_recv.at[0, g], to_right)
            start(7, g, block, block, x_recv.at[1, g], to_left)
        elif what == "x2y":
            whole(r_ref.at[:, left, bins], x_recv.at[0, g])
            block = r_ref.at[0, left, bins]
            start(8, g, block, block, x_recv.at[4, g], to_right)
            whole(r_ref.at[:, right, bins], x_recv.at[1, g])
            block = r_ref.at[1, right, bins]
            start(9, g, block, block, x_recv.at[5, g], to_left)
        elif what == "ey":
            for k in range(2):
                whole(r_ref.at[k, far, bins], x_recv.at[4 + k, g])
        elif what == "zx":
            block = t_ref.at[x, bins]
            whole(block, z_recv.at[0, g])
            start(6, g, block, block, x_recv.at[0, g], to_right)
            start(7, g, block, block, x_recv.at[1, g], to_left)
            block = part(y_hi, x, bins, y_lo)
            whole(block, z_recv.at[1, g])
            start(8, g, block, block, x_recv.at[2, g], to_right)
            start(9, g, block, block, x_recv.at[3, g], to_left)
        elif what == "x2x":
            block = t_ref.at[left, bins]
            whole(block, x_recv.at[0, g])
            start(10, g, block, block, x_recv.at[4, g], to_right)
            block = part(y_hi, right, bins, y_lo)
            whole(block, x_recv.at[3, g])
            start(11, g, block, block, x_recv.at[5, g], to_left)
        elif what == "y1":
            whole(t_ref.at[right, bins], x_recv.at[1, g])
            whole(part(y_hi, left, bins, y_lo), x_recv.at[2, g])
            whole(t_ref.at[far, bins], x_recv.at[4, g])
            whole(part(y_hi, far, bins, y_lo), x_recv.at[5, g])
            along_y_far(g, bins, slice(None))
            along_y(g, bins, slice(None))
        elif what == "ex":
            wait_y(g, bins, slice(None))

    for what, g in ORDER:
        act(what, g)
    whole(s_ref.at[pl.ds(0, WIN - 2)], z_send)
    for copy in started:
        copy.wait_send()


def gathered_spectra(raw, offsets, quality):
    n = len(GROUPS)
    inputs = [pltpu.with_memory_space_constraint(a, pltpu.HBM) for a in (offsets, quality, jnp.asarray(table_seeds()), raw)]
    return pl.pallas_call(
        gather_kernel,
        out_shape=jax.ShapeDtypeStruct((2, X_SIZE, BINS, WIN, 8, LANES), jnp.bfloat16),
        in_specs=[pl.BlockSpec(memory_space=pltpu.HBM)] * 4,
        out_specs=pl.BlockSpec(memory_space=pltpu.VMEM),
        scratch_shapes=[
            pltpu.VMEM((WIN, BINS, 8, LANES), jnp.bfloat16),
            pltpu.VMEM((X_SIZE, BINS, COLUMN, 8, LANES), jnp.bfloat16),
            pltpu.SemaphoreType.DMA,
            pltpu.SemaphoreType.DMA((12, n)),
            pltpu.SemaphoreType.DMA((2, n)),
            pltpu.SemaphoreType.DMA((3, n)),
            pltpu.SemaphoreType.DMA((6, n)),
            pltpu.SMEM((LOCAL_W,), jnp.int32),
            pltpu.VMEM((LOCAL_W, LANES), jnp.int32),
            pltpu.VMEM((4, F, LANES), jnp.float32),
            pltpu.VMEM((2 * F, L), jnp.bfloat16),
            pltpu.VMEM((LOCAL_W, SEG, LANES), jnp.bfloat16),
            pltpu.VMEM((2, SEG, LANES), jnp.float32),
            pltpu.VMEM((2, L, 2 * LANES), jnp.bfloat16),
            pltpu.VMEM((2 * F, 2 * LANES), jnp.float32),
            pltpu.VMEM((F * 8, LANES), jnp.float32),
            pltpu.SemaphoreType.DMA((LOCAL_W + 3,)),
        ],
        compiler_params=pltpu.CompilerParams(
            collective_id=0, has_side_effects=True, vmem_limit_bytes=40 << 20),
        name="gather",
    )(*inputs)


def stack_kernel(r_ref, out_hbm, out_ref, out_sem):
    chan = lax.axis_index("chan")
    row = lax.broadcasted_iota(jnp.int32, (WIN, 8, LANES), 1)
    scale = 1.0 / math.sqrt(WINDOWS)

    def one_bin(f, carry):
        own = r_ref[chan, f].astype(jnp.float32)
        turned = pltpu.roll(own.reshape(WIN, 8, LANES), 4, 1)
        turned = jnp.where(row < 4, turned, -turned).reshape(WIN * 8, LANES)
        ours = jnp.concatenate([own.T, turned.T], 0).astype(jnp.bfloat16)
        for k in range(0, CHAN, 2):
            pair = jnp.concatenate([r_ref[k, f], r_ref[k + 1, f]], 1)
            both = jnp.dot(ours, pair, preferred_element_type=jnp.float32) * scale
            lanes = slice(k * LANES, (k + 2) * LANES)
            out_ref[f, 0, :, lanes] = both[:LANES].astype(jnp.bfloat16)
            out_ref[f, 1, :, lanes] = both[LANES:].astype(jnp.bfloat16)
        pltpu.make_async_copy(out_ref.at[f], out_hbm.at[f], out_sem.at[f]).start()
        return carry

    lax.fori_loop(0, BINS, one_bin, 0)
    for f in range(BINS):
        pltpu.make_async_copy(out_ref.at[f], out_hbm.at[f], out_sem.at[f]).wait()


def stacked(r):
    return pl.pallas_call(
        stack_kernel,
        out_shape=jax.ShapeDtypeStruct((BINS, 2, LANES, C), jnp.bfloat16),
        in_specs=[pl.BlockSpec(memory_space=pltpu.VMEM)],
        out_specs=pl.BlockSpec(memory_space=pl.ANY),
        scratch_shapes=[
            pltpu.VMEM((BINS, 2, LANES, C), jnp.bfloat16),
            pltpu.SemaphoreType.DMA((BINS,)),
        ],
        compiler_params=pltpu.CompilerParams(vmem_limit_bytes=24 << 20),
        name="stack",
    )(r)


def local(raw, offsets, quality):
    r = gathered_spectra(raw, offsets, quality)
    return stacked(r.reshape(CHAN, BINS, WIN * 8, LANES))


def solution(mesh):
    in_specs = (P("win", None, "chan"), P("win"), P("win", "chan"))
    out_specs = P("win", None, "chan", None)
    return jax.shard_map(local, mesh=mesh, in_specs=in_specs, out_specs=out_specs, check_vma=False)
```

```python
import math

import jax
import jax.numpy as jnp
import numpy as np
from jax import lax
from jax.experimental import pallas as pl
from jax.experimental.pallas import tpu as pltpu
from jax.sharding import PartitionSpec as P

C = 1024
F = 384
L = 3072
FIRST_BIN = 60
WINDOWS = 128
SEG = 3200
EPSILON = 1e-05

LANES = 128
LOCAL_W = 4
BINS = 12
X_SIZE, Y_SIZE, Z_SIZE = 4, 4, 8
COLUMN = 2 * Z_SIZE
CHAN, WIN = 8, 32
GROUPS = (('p', 0, 1), ('p', 1, 1), ('p', 2, 1), ('y', 3, 1), ('x', 4, 1), ('y', 5, 1), ('y', 6, 1), ('y', 7, 2), ('y', 9, 3))
ORDER = (
    ("x2p", 0), ("zy", 3), ("x2p", 1), ("zx", 4), ("zy", 5), ("x2p", 2),
    ("yx", 3), ("x2x", 4), ("zp", 0), ("zy", 6), ("zp", 1), ("zp", 2),
    ("zy", 7), ("yx", 5), ("yx", 6), ("y1", 4), ("x2y", 3), ("x2y", 5),
    ("yx", 7), ("zy", 8), ("y1", 0), ("x2y", 6), ("yx", 8), ("x2y", 7),
    ("ex", 4), ("ey", 5), ("y1", 1), ("y1", 2), ("x2y", 8), ("ey", 7),
    ("ey", 3), ("ex", 0), ("ex", 2), ("ey", 6), ("ex", 1), ("ey", 8),
)
MESH = pl.DeviceIdType.MESH


def table_seeds():
    bins = FIRST_BIN + np.arange(F, dtype=np.int64)
    first = 2.0 * math.pi / L * (bins[:, None] * np.arange(LANES)[None, :] % L)
    turn = 2.0 * math.pi / L * (bins * LANES % L)
    turn = np.broadcast_to(turn[:, None], (F, LANES))
    return np.stack([np.cos(first), -np.sin(first), np.cos(turn), -np.sin(turn)]).astype(np.float32)


def spectra_kernel(off_hbm, quality_hbm, seeds_hbm, raw_hbm, s_ref,
                   off_ref, quality_ref, seeds, table, rows, wide, pairs, product, mixed, sem):
    seeds_copy = pltpu.make_async_copy(seeds_hbm, seeds, sem.at[LOCAL_W])
    small = [pltpu.make_async_copy(off_hbm, off_ref, sem.at[LOCAL_W + 1]),
             pltpu.make_async_copy(quality_hbm, quality_ref, sem.at[LOCAL_W + 2])]
    copies = [pltpu.make_async_copy(raw_hbm.at[w], rows.at[w], sem.at[w]) for w in range(LOCAL_W)]
    for copy in [seeds_copy] + small + copies[:1]:
        copy.start()
    seeds_copy.wait()
    for copy in copies[1:]:
        copy.start()

    step, half_blocks = 48, L // LANES // 2
    row = lax.broadcasted_iota(jnp.int32, (step, LANES), 0)
    sign = jnp.where(row % 2 == FIRST_BIN % 2, 1.0, -1.0).astype(jnp.bfloat16)

    def table_rows(i, carry):
        at = pl.multiple_of(i * step, 16)
        c, m = seeds[0, pl.ds(at, step), :], seeds[1, pl.ds(at, step), :]
        tc, tm = seeds[2, pl.ds(at, step), :], seeds[3, pl.ds(at, step), :]
        for a in range(half_blocks):
            for v, first in ((c, at), (m, pl.multiple_of(F + at, 16))):
                v = v.astype(jnp.bfloat16)
                here = pl.ds(first, step)
                table[here, a * LANES:(a + 1) * LANES] = v
                table[here, (a + half_blocks) * LANES:(a + half_blocks + 1) * LANES] = v * sign
            c, m = c * tc - m * tm, m * tc + c * tm
        return carry

    lax.fori_loop(0, F // step, table_rows, 0)
    for copy in small:
        copy.wait()

    def cut(w, lo, hi):
        if lo == 0:
            copies[w].wait()
            wide[w % 2] = rows[w].astype(jnp.float32)
        lanes = slice(w % 2 * LANES, (w % 2 + 1) * LANES)
        pairs[w // 2, lo:hi, lanes] = wide[w % 2, pl.ds(off_ref[w] + lo, hi - lo), :].astype(jnp.bfloat16)

    cut(0, 0, L)
    cut(1, 0, L)
    for first in range(0, LOCAL_W, 2):
        chunk, tile = L // 3, 2 * F // 6
        for i in range(6):
            at = slice(i * tile, (i + 1) * tile)
            product[at] = jnp.dot(table[at], pairs[first // 2], preferred_element_type=jnp.float32)
            if first + 2 < LOCAL_W:
                cut(first + 2 + i // 3, i % 3 * chunk, (i % 3 + 1) * chunk)
        power = jnp.sum(product[...] * product[...], axis=0, keepdims=True) / F
        whiten = lax.rsqrt(power + EPSILON)
        for half in range(2):
            w = first + half
            lanes = slice(half * LANES, (half + 1) * LANES)
            gain = whiten[:, lanes] * quality_ref[w:w + 1, :].astype(jnp.float32)
            for p in range(2):
                mixed[pl.ds(p * LOCAL_W + w, F, stride=8), :] = product[p * F:(p + 1) * F, lanes] * gain
    s_ref[...] = mixed[...].astype(jnp.bfloat16).reshape(2, COLUMN, BINS, 8, LANES)


def gather_kernel(off_hbm, quality_hbm, seeds_hbm, raw_hbm, r_ref,
                  s_ref, t_ref, p_ref, z_send, send_sem, z_recv, y_recv, x_recv, p_sem, own_sem, *spectra_scratch):
    def spectra():
        spectra_kernel(off_hbm, quality_hbm, seeds_hbm, raw_hbm, s_ref, *spectra_scratch)

    chan, win = lax.axis_index("chan"), lax.axis_index("win")
    y_hi, x = chan // X_SIZE, chan % X_SIZE
    y_lo, spot = win // COLUMN, win % COLUMN
    y = y_hi * 2 + y_lo
    left, right, far = (x + 3) % X_SIZE, (x + 1) % X_SIZE, (x + 2) % X_SIZE

    def column(i):
        return chan, y_lo * COLUMN + i

    def at_y(step):
        other = (y + step) % Y_SIZE
        return (other // 2) * X_SIZE + x, (other % 2) * COLUMN + spot

    to_right, to_left, to_up, to_down = (y_hi * X_SIZE + right, win), (y_hi * X_SIZE + left, win), at_y(1), at_y(3)

    def other_spot(d):
        return (spot + d) % COLUMN

    order = [d for k in range(1, COLUMN // 2) for d in (k, COLUMN - k)] + [COLUMN // 2]
    peers = [column(other_spot(d)) for d in order] + [to_up, to_down, at_y(2), to_right, to_left]
    barrier = pltpu.get_barrier_semaphore()
    for peer in peers:
        pl.semaphore_signal(barrier, inc=1, device_id=peer, device_id_type=MESH)

    spectra()
    pl.semaphore_wait(barrier, len(peers))

    def remote(src, dst, send, recv, peer):
        return pltpu.make_async_remote_copy(
            src_ref=src, dst_ref=dst, send_sem=send, recv_sem=recv, device_id=peer, device_id_type=MESH)

    started = []

    def start(k, g, src, dst, recv, peer):
        copy = remote(src, dst, send_sem.at[k, g], recv, peer)
        copy.start()
        started.append(copy)

    def whole(ref, sem):
        pltpu.make_async_copy(ref, ref, sem).wait()

    spans = [pl.ds(first, count) for _, first, count in GROUPS]

    def along_z(source, landing, send, g):
        pltpu.make_async_copy(source(spot), landing, z_recv.at[g]).start()

        def spread(d):
            i = other_spot(d)
            remote(source(i), landing, send, z_recv.at[g], column(i)).start()

        def both_ways(k, carry):
            spread(k)
            spread(COLUMN - k)
            return carry

        lax.fori_loop(1, COLUMN // 2, both_ways, 0)
        spread(COLUMN // 2)

    every = slice(None)
    early = 0
    for g, bins in enumerate(spans):
        if GROUPS[g][0] == "p":
            early += GROUPS[g][2]
            block = s_ref.at[:, :, bins]
            start(6, g, block, p_ref.at[x, :, :, bins], x_recv.at[0, g], to_right)
            start(7, g, block, p_ref.at[x, :, :, bins], x_recv.at[1, g], to_left)
            pltpu.make_async_copy(block, p_ref.at[x, :, :, bins], p_sem.at[0, g]).start()
    for g, bins in enumerate(spans):
        if GROUPS[g][0] != "p":
            along_z(lambda i: s_ref.at[:, i, bins], t_ref.at[x, :, bins, spot], z_send, g)

    def part(chan_y, xs, bins, lo):
        return r_ref.at[chan_y, xs, bins, pl.ds(lo * COLUMN, COLUMN)]

    def along_y(g, bins, xs):
        landing = part(y_hi, xs, bins, y_lo)
        other, own = t_ref.at[xs, 1 - y_lo, bins], t_ref.at[xs, y_lo, bins]
        start(0, g, other, landing, y_recv.at[0, g], to_up)
        start(1, g, other, landing, y_recv.at[1, g], to_down)
        start(2, g, own, landing, y_recv.at[2, g], at_y(2))
        pltpu.make_async_copy(own, landing, own_sem.at[g]).start()

    def wait_y(g, bins, xs):
        for k, step in ((0, 3), (1, 1), (2, 2)):
            other = (y + step) % Y_SIZE
            whole(part(other // 2, xs, bins, other % 2), y_recv.at[k, g])
        whole(part(y_hi, xs, bins, y_lo), own_sem.at[g])

    def act(what, g):
        bins = spans[g]
        if what == "zy":
            whole(t_ref.at[x, :, bins], z_recv.at[g])
            along_y(g, bins, x)
        elif what == "yx":
            wait_y(g, bins, x)
            block = r_ref.at[:, x, bins]
            start(6, g, block, block, x_recv.at[0, g], to_right)
            start(7, g, block, block, x_recv.at[1, g], to_left)
        elif what == "x2y":
            whole(r_ref.at[:, left, bins], x_recv.at[0, g])
            block = r_ref.at[0, left, bins]
            start(8, g, block, block, x_recv.at[2, g], to_right)
            whole(r_ref.at[:, right, bins], x_recv.at[1, g])
            block = r_ref.at[1, right, bins]
            start(9, g, block, block, x_recv.at[3, g], to_left)
        elif what == "ey":
            for k in range(2):
                whole(r_ref.at[k, far, bins], x_recv.at[2 + k, g])
        elif what == "zx":
            block = t_ref.at[x, :, bins]
            whole(block, z_recv.at[g])
            start(6, g, block, block, x_recv.at[0, g], to_right)
            start(7, g, block, block, x_recv.at[1, g], to_left)
        elif what == "x2x":
            whole(t_ref.at[left, :, bins], x_recv.at[0, g])
            block = t_ref.at[left, 0, bins]
            start(8, g, block, block, x_recv.at[2, g], to_right)
            whole(t_ref.at[right, :, bins], x_recv.at[1, g])
            block = t_ref.at[right, 1, bins]
            start(9, g, block, block, x_recv.at[3, g], to_left)
        elif what == "x2p":
            whole(p_ref.at[left, :, :, bins], x_recv.at[0, g])
            block = p_ref.at[left, 0, :, bins]
            start(8, g, block, block, x_recv.at[2, g], to_right)
            whole(p_ref.at[right, :, :, bins], x_recv.at[1, g])
            block = p_ref.at[right, 1, :, bins]
            start(9, g, block, block, x_recv.at[3, g], to_left)
        elif what == "zp":
            whole(p_ref.at[x, :, :, bins], p_sem.at[0, g])
            for k in range(2):
                whole(p_ref.at[far, k, :, bins], x_recv.at[2 + k, g])
            along_z(lambda i: p_ref.at[:, :, i, bins], t_ref.at[:, :, bins, spot], p_sem.at[1, g], g)
        elif what == "y1":
            if GROUPS[g][0] == "p":
                whole(t_ref.at[:, :, bins], z_recv.at[g])
            else:
                for k in range(2):
                    whole(t_ref.at[far, k, bins], x_recv.at[2 + k, g])
            along_y(g, bins, every)
        elif what == "ex":
            wait_y(g, bins, every)

    for what, g in ORDER:
        act(what, g)
    whole(s_ref.at[:, pl.ds(0, COLUMN - 1), pl.ds(0, BINS - early)], z_send)
    for g, bins in enumerate(spans):
        if GROUPS[g][0] == "p":
            whole(p_ref.at[:, :, pl.ds(0, COLUMN - 1), bins], p_sem.at[1, g])
    for copy in started:
        copy.wait_send()


def gathered_spectra(raw, offsets, quality):
    n = len(GROUPS)
    inputs = [pltpu.with_memory_space_constraint(a, pltpu.HBM) for a in (offsets, quality, jnp.asarray(table_seeds()), raw)]
    return pl.pallas_call(
        gather_kernel,
        out_shape=jax.ShapeDtypeStruct((2, X_SIZE, BINS, WIN, 8, LANES), jnp.bfloat16),
        in_specs=[pl.BlockSpec(memory_space=pltpu.HBM)] * 4,
        out_specs=pl.BlockSpec(memory_space=pltpu.VMEM),
        scratch_shapes=[
            pltpu.VMEM((2, COLUMN, BINS, 8, LANES), jnp.bfloat16),
            pltpu.VMEM((X_SIZE, 2, BINS, COLUMN, 8, LANES), jnp.bfloat16),
            pltpu.VMEM((X_SIZE, 2, COLUMN, BINS, 8, LANES), jnp.bfloat16),
            pltpu.SemaphoreType.DMA,
            pltpu.SemaphoreType.DMA((10, n)),
            pltpu.SemaphoreType.DMA((n,)),
            pltpu.SemaphoreType.DMA((3, n)),
            pltpu.SemaphoreType.DMA((4, n)),
            pltpu.SemaphoreType.DMA((2, n)),
            pltpu.SemaphoreType.DMA((n,)),
            pltpu.SMEM((LOCAL_W,), jnp.int32),
            pltpu.VMEM((LOCAL_W, LANES), jnp.int32),
            pltpu.VMEM((4, F, LANES), jnp.float32),
            pltpu.VMEM((2 * F, L), jnp.bfloat16),
            pltpu.VMEM((LOCAL_W, SEG, LANES), jnp.bfloat16),
            pltpu.VMEM((2, SEG, LANES), jnp.float32),
            pltpu.VMEM((2, L, 2 * LANES), jnp.bfloat16),
            pltpu.VMEM((2 * F, 2 * LANES), jnp.float32),
            pltpu.VMEM((F * 8, LANES), jnp.float32),
            pltpu.SemaphoreType.DMA((LOCAL_W + 3,)),
        ],
        compiler_params=pltpu.CompilerParams(
            collective_id=0, has_side_effects=True, vmem_limit_bytes=40 << 20),
        name="gather",
    )(*inputs)


def stack_kernel(r_ref, out_hbm, out_ref, out_sem):
    chan = lax.axis_index("chan")
    row = lax.broadcasted_iota(jnp.int32, (WIN, 8, LANES), 1)
    scale = 1.0 / math.sqrt(WINDOWS)

    def one_bin(f, carry):
        own = r_ref[chan, f].astype(jnp.float32)
        turned = pltpu.roll(own.reshape(WIN, 8, LANES), 4, 1)
        turned = jnp.where(row < 4, turned, -turned).reshape(WIN * 8, LANES)
        ours = jnp.concatenate([own.T, turned.T], 0).astype(jnp.bfloat16)
        for k in range(0, CHAN, 2):
            pair = jnp.concatenate([r_ref[k, f], r_ref[k + 1, f]], 1)
            both = jnp.dot(ours, pair, preferred_element_type=jnp.float32) * scale
            lanes = slice(k * LANES, (k + 2) * LANES)
            out_ref[f, 0, :, lanes] = both[:LANES].astype(jnp.bfloat16)
            out_ref[f, 1, :, lanes] = both[LANES:].astype(jnp.bfloat16)
        pltpu.make_async_copy(out_ref.at[f], out_hbm.at[f], out_sem.at[f]).start()
        return carry

    lax.fori_loop(0, BINS, one_bin, 0)
    for f in range(BINS):
        pltpu.make_async_copy(out_ref.at[f], out_hbm.at[f], out_sem.at[f]).wait()


def stacked(r):
    return pl.pallas_call(
        stack_kernel,
        out_shape=jax.ShapeDtypeStruct((BINS, 2, LANES, C), jnp.bfloat16),
        in_specs=[pl.BlockSpec(memory_space=pltpu.VMEM)],
        out_specs=pl.BlockSpec(memory_space=pl.ANY),
        scratch_shapes=[
            pltpu.VMEM((BINS, 2, LANES, C), jnp.bfloat16),
            pltpu.SemaphoreType.DMA((BINS,)),
        ],
        compiler_params=pltpu.CompilerParams(vmem_limit_bytes=24 << 20),
        name="stack",
    )(r)


def local(raw, offsets, quality):
    r = gathered_spectra(raw, offsets, quality)
    return stacked(r.reshape(CHAN, BINS, WIN * 8, LANES))


def solution(mesh):
    in_specs = (P("win", None, "chan"), P("win"), P("win", "chan"))
    out_specs = P("win", None, "chan", None)
    return jax.shard_map(local, mesh=mesh, in_specs=in_specs, out_specs=out_specs, check_vma=False)
```

```python
import math

import jax
import jax.numpy as jnp
import numpy as np
from jax import lax
from jax.experimental import pallas as pl
from jax.experimental.pallas import tpu as pltpu
from jax.sharding import PartitionSpec as P

C = 1024
F = 384
L = 3072
FIRST_BIN = 60
WINDOWS = 128
SEG = 3200
EPSILON = 1e-05

LANES = 128
LOCAL_W = 4
BINS = 12
X_SIZE, Y_SIZE, Z_SIZE = 4, 4, 8
COLUMN = 2 * Z_SIZE
CHAN, WIN = 8, 32
GROUPS = (('p', 0, 1), ('p', 1, 1), ('p', 2, 1), ('p', 3, 1), ('y', 4, 1), ('y', 5, 1), ('y', 6, 2), ('y', 8, 2), ('y', 10, 2))
ORDER = (
    ("x2p", 0), ("zy", 4), ("x2p", 1), ("zy", 5), ("x2p", 2), ("x2p", 3),
    ("yx", 4), ("zp", 0), ("zy", 6), ("zp", 1), ("yx", 5), ("zp", 2),
    ("zp", 3), ("zy", 7), ("x2y", 4), ("yx", 6), ("zy", 8), ("x2y", 5),
    ("yx", 7), ("yx", 8), ("y1", 0), ("x2y", 6), ("y1", 1), ("x2y", 7),
    ("y1", 2), ("x2y", 8), ("y1", 3), ("ey", 4), ("ey", 5), ("ex", 0),
    ("ex", 1), ("ey", 6), ("ex", 2), ("ey", 7), ("ey", 8), ("ex", 3),
)
MESH = pl.DeviceIdType.MESH


def table_seeds():
    bins = FIRST_BIN + np.arange(F, dtype=np.int64)
    first = 2.0 * math.pi / L * (bins[:, None] * np.arange(LANES)[None, :] % L)
    turn = 2.0 * math.pi / L * (bins * LANES % L)
    turn = np.broadcast_to(turn[:, None], (F, LANES))
    return np.stack([np.cos(first), -np.sin(first), np.cos(turn), -np.sin(turn)]).astype(np.float32)


def spectra_kernel(off_hbm, quality_hbm, seeds_hbm, raw_hbm, s_ref,
                   off_ref, quality_ref, seeds, table, rows, wide, pairs, product, mixed, sem):
    seeds_copy = pltpu.make_async_copy(seeds_hbm, seeds, sem.at[LOCAL_W])
    small = [pltpu.make_async_copy(off_hbm, off_ref, sem.at[LOCAL_W + 1]),
             pltpu.make_async_copy(quality_hbm, quality_ref, sem.at[LOCAL_W + 2])]
    copies = [pltpu.make_async_copy(raw_hbm.at[w], rows.at[w], sem.at[w]) for w in range(LOCAL_W)]
    for copy in [seeds_copy] + small + copies[:1]:
        copy.start()
    seeds_copy.wait()
    for copy in copies[1:]:
        copy.start()

    step, half_blocks = 48, L // LANES // 2
    row = lax.broadcasted_iota(jnp.int32, (step, LANES), 0)
    sign = jnp.where(row % 2 == FIRST_BIN % 2, 1.0, -1.0).astype(jnp.bfloat16)

    def table_rows(i, carry):
        at = pl.multiple_of(i * step, 16)
        c, m = seeds[0, pl.ds(at, step), :], seeds[1, pl.ds(at, step), :]
        tc, tm = seeds[2, pl.ds(at, step), :], seeds[3, pl.ds(at, step), :]
        for a in range(half_blocks):
            for v, first in ((c, at), (m, pl.multiple_of(F + at, 16))):
                v = v.astype(jnp.bfloat16)
                here = pl.ds(first, step)
                table[here, a * LANES:(a + 1) * LANES] = v
                table[here, (a + half_blocks) * LANES:(a + half_blocks + 1) * LANES] = v * sign
            c, m = c * tc - m * tm, m * tc + c * tm
        return carry

    lax.fori_loop(0, F // step, table_rows, 0)
    for copy in small:
        copy.wait()

    def cut(w, lo, hi):
        if lo == 0:
            copies[w].wait()
            wide[w % 2] = rows[w].astype(jnp.float32)
        lanes = slice(w % 2 * LANES, (w % 2 + 1) * LANES)
        pairs[w // 2, lo:hi, lanes] = wide[w % 2, pl.ds(off_ref[w] + lo, hi - lo), :].astype(jnp.bfloat16)

    cut(0, 0, L)
    cut(1, 0, L)
    for first in range(0, LOCAL_W, 2):
        chunk, tile = L // 3, 2 * F // 6
        for i in range(6):
            at = slice(i * tile, (i + 1) * tile)
            product[at] = jnp.dot(table[at], pairs[first // 2], preferred_element_type=jnp.float32)
            if first + 2 < LOCAL_W:
                cut(first + 2 + i // 3, i % 3 * chunk, (i % 3 + 1) * chunk)
        power = jnp.sum(product[...] * product[...], axis=0, keepdims=True) / F
        whiten = lax.rsqrt(power + EPSILON)
        for half in range(2):
            w = first + half
            lanes = slice(half * LANES, (half + 1) * LANES)
            gain = whiten[:, lanes] * quality_ref[w:w + 1, :].astype(jnp.float32)
            for p in range(2):
                mixed[pl.ds(p * LOCAL_W + w, F, stride=8), :] = product[p * F:(p + 1) * F, lanes] * gain
    s_ref[...] = mixed[...].astype(jnp.bfloat16).reshape(2, COLUMN, BINS, 8, LANES)


def gather_kernel(off_hbm, quality_hbm, seeds_hbm, raw_hbm, r_ref,
                  s_ref, t_ref, p_ref, z_send, send_sem, z_recv, y_recv, x_recv, p_sem, own_sem, *spectra_scratch):
    def spectra():
        spectra_kernel(off_hbm, quality_hbm, seeds_hbm, raw_hbm, s_ref, *spectra_scratch)

    chan, win = lax.axis_index("chan"), lax.axis_index("win")
    y_hi, x = chan // X_SIZE, chan % X_SIZE
    y_lo, spot = win // COLUMN, win % COLUMN
    y = y_hi * 2 + y_lo
    left, right, far = (x + 3) % X_SIZE, (x + 1) % X_SIZE, (x + 2) % X_SIZE

    def column(i):
        return chan, y_lo * COLUMN + i

    def at_y(step):
        other = (y + step) % Y_SIZE
        return (other // 2) * X_SIZE + x, (other % 2) * COLUMN + spot

    to_right, to_left, to_up, to_down = (y_hi * X_SIZE + right, win), (y_hi * X_SIZE + left, win), at_y(1), at_y(3)

    def other_spot(d):
        return (spot + d) % COLUMN

    order = [d for k in range(1, COLUMN // 2) for d in (k, COLUMN - k)] + [COLUMN // 2]
    peers = [column(other_spot(d)) for d in order] + [to_up, to_down, at_y(2), to_right, to_left]
    barrier = pltpu.get_barrier_semaphore()
    for peer in peers:
        pl.semaphore_signal(barrier, inc=1, device_id=peer, device_id_type=MESH)

    spectra()
    pl.semaphore_wait(barrier, len(peers))

    def remote(src, dst, send, recv, peer):
        return pltpu.make_async_remote_copy(
            src_ref=src, dst_ref=dst, send_sem=send, recv_sem=recv, device_id=peer, device_id_type=MESH)

    started = []

    def start(k, g, src, dst, recv, peer):
        copy = remote(src, dst, send_sem.at[k, g], recv, peer)
        copy.start()
        started.append(copy)

    def whole(ref, sem):
        pltpu.make_async_copy(ref, ref, sem).wait()

    spans = [pl.ds(first, count) for _, first, count in GROUPS]

    def along_z(source, landing, send, g):
        pltpu.make_async_copy(source(spot), landing, z_recv.at[g]).start()

        def spread(d):
            i = other_spot(d)
            remote(source(i), landing, send, z_recv.at[g], column(i)).start()

        def both_ways(k, carry):
            spread(k)
            spread(COLUMN - k)
            return carry

        lax.fori_loop(1, COLUMN // 2, both_ways, 0)
        spread(COLUMN // 2)

    every = slice(None)
    early = 0
    for g, bins in enumerate(spans):
        if GROUPS[g][0] == "p":
            early += GROUPS[g][2]
            block = s_ref.at[:, :, bins]
            start(6, g, block, p_ref.at[x, :, :, bins], x_recv.at[0, g], to_right)
            start(7, g, block, p_ref.at[x, :, :, bins], x_recv.at[1, g], to_left)
            pltpu.make_async_copy(block, p_ref.at[x, :, :, bins], p_sem.at[0, g]).start()
    for g, bins in enumerate(spans):
        if GROUPS[g][0] != "p":
            along_z(lambda i: s_ref.at[:, i, bins], t_ref.at[x, :, bins, spot], z_send, g)

    def part(chan_y, xs, bins, lo):
        return r_ref.at[chan_y, xs, bins, pl.ds(lo * COLUMN, COLUMN)]

    def along_y(g, bins, xs):
        landing = part(y_hi, xs, bins, y_lo)
        other, own = t_ref.at[xs, 1 - y_lo, bins], t_ref.at[xs, y_lo, bins]
        start(0, g, other, landing, y_recv.at[0, g], to_up)
        start(1, g, other, landing, y_recv.at[1, g], to_down)
        start(2, g, own, landing, y_recv.at[2, g], at_y(2))
        pltpu.make_async_copy(own, landing, own_sem.at[g]).start()

    def wait_y(g, bins, xs):
        for k, step in ((0, 3), (1, 1), (2, 2)):
            other = (y + step) % Y_SIZE
            whole(part(other // 2, xs, bins, other % 2), y_recv.at[k, g])
        whole(part(y_hi, xs, bins, y_lo), own_sem.at[g])

    def act(what, g):
        bins = spans[g]
        if what == "zy":
            whole(t_ref.at[x, :, bins], z_recv.at[g])
            along_y(g, bins, x)
        elif what == "yx":
            wait_y(g, bins, x)
            block = r_ref.at[:, x, bins]
            start(6, g, block, block, x_recv.at[0, g], to_right)
            start(7, g, block, block, x_recv.at[1, g], to_left)
        elif what == "x2y":
            whole(r_ref.at[:, left, bins], x_recv.at[0, g])
            block = r_ref.at[0, left, bins]
            start(8, g, block, block, x_recv.at[2, g], to_right)
            whole(r_ref.at[:, right, bins], x_recv.at[1, g])
            block = r_ref.at[1, right, bins]
            start(9, g, block, block, x_recv.at[3, g], to_left)
        elif what == "ey":
            for k in range(2):
                whole(r_ref.at[k, far, bins], x_recv.at[2 + k, g])
        elif what == "zx":
            block = t_ref.at[x, :, bins]
            whole(block, z_recv.at[g])
            start(6, g, block, block, x_recv.at[0, g], to_right)
            start(7, g, block, block, x_recv.at[1, g], to_left)
        elif what == "x2x":
            whole(t_ref.at[left, :, bins], x_recv.at[0, g])
            block = t_ref.at[left, 0, bins]
            start(8, g, block, block, x_recv.at[2, g], to_right)
            whole(t_ref.at[right, :, bins], x_recv.at[1, g])
            block = t_ref.at[right, 1, bins]
            start(9, g, block, block, x_recv.at[3, g], to_left)
        elif what == "x2p":
            whole(p_ref.at[left, :, :, bins], x_recv.at[0, g])
            block = p_ref.at[left, 0, :, bins]
            start(8, g, block, block, x_recv.at[2, g], to_right)
            whole(p_ref.at[right, :, :, bins], x_recv.at[1, g])
            block = p_ref.at[right, 1, :, bins]
            start(9, g, block, block, x_recv.at[3, g], to_left)
        elif what == "zp":
            whole(p_ref.at[x, :, :, bins], p_sem.at[0, g])
            for k in range(2):
                whole(p_ref.at[far, k, :, bins], x_recv.at[2 + k, g])
            along_z(lambda i: p_ref.at[:, :, i, bins], t_ref.at[:, :, bins, spot], p_sem.at[1, g], g)
        elif what == "y1":
            if GROUPS[g][0] == "p":
                whole(t_ref.at[:, :, bins], z_recv.at[g])
            else:
                for k in range(2):
                    whole(t_ref.at[far, k, bins], x_recv.at[2 + k, g])
            along_y(g, bins, every)
        elif what == "ex":
            wait_y(g, bins, every)

    for what, g in ORDER:
        act(what, g)
    whole(s_ref.at[:, pl.ds(0, COLUMN - 1), pl.ds(0, BINS - early)], z_send)
    for g, bins in enumerate(spans):
        if GROUPS[g][0] == "p":
            whole(p_ref.at[:, :, pl.ds(0, COLUMN - 1), bins], p_sem.at[1, g])
    for copy in started:
        copy.wait_send()


def gathered_spectra(raw, offsets, quality):
    n = len(GROUPS)
    inputs = [pltpu.with_memory_space_constraint(a, pltpu.HBM) for a in (offsets, quality, jnp.asarray(table_seeds()), raw)]
    return pl.pallas_call(
        gather_kernel,
        out_shape=jax.ShapeDtypeStruct((2, X_SIZE, BINS, WIN, 8, LANES), jnp.bfloat16),
        in_specs=[pl.BlockSpec(memory_space=pltpu.HBM)] * 4,
        out_specs=pl.BlockSpec(memory_space=pltpu.VMEM),
        scratch_shapes=[
            pltpu.VMEM((2, COLUMN, BINS, 8, LANES), jnp.bfloat16),
            pltpu.VMEM((X_SIZE, 2, BINS, COLUMN, 8, LANES), jnp.bfloat16),
            pltpu.VMEM((X_SIZE, 2, COLUMN, BINS, 8, LANES), jnp.bfloat16),
            pltpu.SemaphoreType.DMA,
            pltpu.SemaphoreType.DMA((10, n)),
            pltpu.SemaphoreType.DMA((n,)),
            pltpu.SemaphoreType.DMA((3, n)),
            pltpu.SemaphoreType.DMA((4, n)),
            pltpu.SemaphoreType.DMA((2, n)),
            pltpu.SemaphoreType.DMA((n,)),
            pltpu.SMEM((LOCAL_W,), jnp.int32),
            pltpu.VMEM((LOCAL_W, LANES), jnp.int32),
            pltpu.VMEM((4, F, LANES), jnp.float32),
            pltpu.VMEM((2 * F, L), jnp.bfloat16),
            pltpu.VMEM((LOCAL_W, SEG, LANES), jnp.bfloat16),
            pltpu.VMEM((2, SEG, LANES), jnp.float32),
            pltpu.VMEM((2, L, 2 * LANES), jnp.bfloat16),
            pltpu.VMEM((2 * F, 2 * LANES), jnp.float32),
            pltpu.VMEM((F * 8, LANES), jnp.float32),
            pltpu.SemaphoreType.DMA((LOCAL_W + 3,)),
        ],
        compiler_params=pltpu.CompilerParams(
            collective_id=0, has_side_effects=True, vmem_limit_bytes=40 << 20),
        name="gather",
    )(*inputs)


def stack_kernel(r_ref, out_hbm, out_ref, out_sem):
    chan = lax.axis_index("chan")
    row = lax.broadcasted_iota(jnp.int32, (WIN, 8, LANES), 1)
    scale = 1.0 / math.sqrt(WINDOWS)

    def one_bin(f, carry):
        own = r_ref[chan, f].astype(jnp.float32)
        turned = pltpu.roll(own.reshape(WIN, 8, LANES), 4, 1)
        turned = jnp.where(row < 4, turned, -turned).reshape(WIN * 8, LANES)
        ours = jnp.concatenate([own.T, turned.T], 0).astype(jnp.bfloat16)
        for k in range(0, CHAN, 2):
            pair = jnp.concatenate([r_ref[k, f], r_ref[k + 1, f]], 1)
            both = jnp.dot(ours, pair, preferred_element_type=jnp.float32) * scale
            lanes = slice(k * LANES, (k + 2) * LANES)
            out_ref[f, 0, :, lanes] = both[:LANES].astype(jnp.bfloat16)
            out_ref[f, 1, :, lanes] = both[LANES:].astype(jnp.bfloat16)
        pltpu.make_async_copy(out_ref.at[f], out_hbm.at[f], out_sem.at[f]).start()
        return carry

    lax.fori_loop(0, BINS, one_bin, 0, unroll=6)
    for f in range(BINS):
        pltpu.make_async_copy(out_ref.at[f], out_hbm.at[f], out_sem.at[f]).wait()


def stacked(r):
    return pl.pallas_call(
        stack_kernel,
        out_shape=jax.ShapeDtypeStruct((BINS, 2, LANES, C), jnp.bfloat16),
        in_specs=[pl.BlockSpec(memory_space=pltpu.VMEM)],
        out_specs=pl.BlockSpec(memory_space=pl.ANY),
        scratch_shapes=[
            pltpu.VMEM((BINS, 2, LANES, C), jnp.bfloat16),
            pltpu.SemaphoreType.DMA((BINS,)),
        ],
        compiler_params=pltpu.CompilerParams(vmem_limit_bytes=24 << 20),
        name="stack",
    )(r)


def local(raw, offsets, quality):
    r = gathered_spectra(raw, offsets, quality)
    return stacked(r.reshape(CHAN, BINS, WIN * 8, LANES))


def solution(mesh):
    in_specs = (P("win", None, "chan"), P("win"), P("win", "chan"))
    out_specs = P("win", None, "chan", None)
    return jax.shard_map(local, mesh=mesh, in_specs=in_specs, out_specs=out_specs, check_vma=False)
```

```python
import math

import jax
import jax.numpy as jnp
import numpy as np
from jax import lax
from jax.experimental import pallas as pl
from jax.experimental.pallas import tpu as pltpu
from jax.sharding import PartitionSpec as P

C = 1024
F = 384
L = 3072
FIRST_BIN = 60
WINDOWS = 128
SEG = 3200
EPSILON = 1e-05

LANES = 128
LOCAL_W = 4
BINS = 12
X_SIZE, Y_SIZE, Z_SIZE = 4, 4, 8
COLUMN = 2 * Z_SIZE
CHAN, WIN = 8, 32
GROUPS = (('p', 0, 1), ('p', 1, 1), ('p', 2, 1), ('p', 3, 1), ('y', 4, 1), ('y', 5, 2), ('y', 7, 3), ('y', 10, 2))
ORDER = (
    ("x2p", 0), ("zy", 4), ("x2p", 1), ("x2p", 2), ("zy", 5), ("x2p", 3),
    ("yx", 4), ("zp", 0), ("zp", 1), ("zp", 2), ("zp", 3), ("zy", 6),
    ("yx", 5), ("x2y", 4), ("zy", 7), ("yx", 6), ("x2y", 5), ("y1", 0),
    ("yx", 7), ("y1", 1), ("x2y", 6), ("y1", 2), ("y1", 3), ("x2y", 7),
    ("ey", 4), ("ex", 0), ("ey", 5), ("ex", 1), ("ex", 2), ("ey", 6),
    ("ey", 7), ("ex", 3),
)
MESH = pl.DeviceIdType.MESH


def table_seeds():
    bins = FIRST_BIN + np.arange(F, dtype=np.int64)
    first = 2.0 * math.pi / L * (bins[:, None] * np.arange(LANES)[None, :] % L)
    turn = 2.0 * math.pi / L * (bins * LANES % L)
    turn = np.broadcast_to(turn[:, None], (F, LANES))
    return np.stack([np.cos(first), -np.sin(first), np.cos(turn), -np.sin(turn)]).astype(np.float32)


def spectra_kernel(off_hbm, quality_hbm, seeds_hbm, raw_hbm, s_ref,
                   off_ref, quality_ref, seeds, table, rows, wide, pairs, product, mixed, sem):
    seeds_copy = pltpu.make_async_copy(seeds_hbm, seeds, sem.at[LOCAL_W])
    small = [pltpu.make_async_copy(off_hbm, off_ref, sem.at[LOCAL_W + 1]),
             pltpu.make_async_copy(quality_hbm, quality_ref, sem.at[LOCAL_W + 2])]
    copies = [pltpu.make_async_copy(raw_hbm.at[w], rows.at[w], sem.at[w]) for w in range(LOCAL_W)]
    for copy in [seeds_copy] + small + copies[:1]:
        copy.start()
    seeds_copy.wait()
    for copy in copies[1:]:
        copy.start()

    step, half_blocks = 48, L // LANES // 2
    row = lax.broadcasted_iota(jnp.int32, (step, LANES), 0)
    sign = jnp.where(row % 2 == FIRST_BIN % 2, 1.0, -1.0).astype(jnp.bfloat16)

    def table_rows(i, carry):
        at = pl.multiple_of(i * step, 16)
        c, m = seeds[0, pl.ds(at, step), :], seeds[1, pl.ds(at, step), :]
        tc, tm = seeds[2, pl.ds(at, step), :], seeds[3, pl.ds(at, step), :]
        for a in range(half_blocks):
            for v, first in ((c, at), (m, pl.multiple_of(F + at, 16))):
                v = v.astype(jnp.bfloat16)
                here = pl.ds(first, step)
                table[here, a * LANES:(a + 1) * LANES] = v
                table[here, (a + half_blocks) * LANES:(a + half_blocks + 1) * LANES] = v * sign
            c, m = c * tc - m * tm, m * tc + c * tm
        return carry

    lax.fori_loop(0, F // step, table_rows, 0)
    for copy in small:
        copy.wait()

    def cut(w, lo, hi):
        if lo == 0:
            copies[w].wait()
            wide[w % 2] = rows[w].astype(jnp.float32)
        lanes = slice(w % 2 * LANES, (w % 2 + 1) * LANES)
        pairs[w // 2, lo:hi, lanes] = wide[w % 2, pl.ds(off_ref[w] + lo, hi - lo), :].astype(jnp.bfloat16)

    cut(0, 0, L)
    cut(1, 0, L)
    for first in range(0, LOCAL_W, 2):
        chunk, tile = L // 3, 2 * F // 6
        for i in range(6):
            at = slice(i * tile, (i + 1) * tile)
            product[at] = jnp.dot(table[at], pairs[first // 2], preferred_element_type=jnp.float32)
            if first + 2 < LOCAL_W:
                cut(first + 2 + i // 3, i % 3 * chunk, (i % 3 + 1) * chunk)
        power = jnp.sum(product[...] * product[...], axis=0, keepdims=True) / F
        whiten = lax.rsqrt(power + EPSILON)
        for half in range(2):
            w = first + half
            lanes = slice(half * LANES, (half + 1) * LANES)
            gain = whiten[:, lanes] * quality_ref[w:w + 1, :].astype(jnp.float32)
            for p in range(2):
                mixed[pl.ds(p * LOCAL_W + w, F, stride=8), :] = product[p * F:(p + 1) * F, lanes] * gain
    s_ref[...] = mixed[...].astype(jnp.bfloat16).reshape(2, COLUMN, BINS, 8, LANES)


def gather_kernel(off_hbm, quality_hbm, seeds_hbm, raw_hbm, r_ref,
                  s_ref, t_ref, p_ref, z_send, send_sem, z_recv, y_recv, x_recv, p_sem, own_sem, *spectra_scratch):
    def spectra():
        spectra_kernel(off_hbm, quality_hbm, seeds_hbm, raw_hbm, s_ref, *spectra_scratch)

    chan, win = lax.axis_index("chan"), lax.axis_index("win")
    y_hi, x = chan // X_SIZE, chan % X_SIZE
    y_lo, spot = win // COLUMN, win % COLUMN
    y = y_hi * 2 + y_lo
    left, right, far = (x + 3) % X_SIZE, (x + 1) % X_SIZE, (x + 2) % X_SIZE

    def column(i):
        return chan, y_lo * COLUMN + i

    def at_y(step):
        other = (y + step) % Y_SIZE
        return (other // 2) * X_SIZE + x, (other % 2) * COLUMN + spot

    to_right, to_left, to_up, to_down = (y_hi * X_SIZE + right, win), (y_hi * X_SIZE + left, win), at_y(1), at_y(3)

    def other_spot(d):
        return (spot + d) % COLUMN

    order = [d for k in range(1, COLUMN // 2) for d in (k, COLUMN - k)] + [COLUMN // 2]
    peers = [column(other_spot(d)) for d in order] + [to_up, to_down, at_y(2), to_right, to_left]
    barrier = pltpu.get_barrier_semaphore()
    for peer in peers:
        pl.semaphore_signal(barrier, inc=1, device_id=peer, device_id_type=MESH)

    spectra()
    pl.semaphore_wait(barrier, len(peers))

    def remote(src, dst, send, recv, peer):
        return pltpu.make_async_remote_copy(
            src_ref=src, dst_ref=dst, send_sem=send, recv_sem=recv, device_id=peer, device_id_type=MESH)

    started = []

    def start(k, g, src, dst, recv, peer):
        copy = remote(src, dst, send_sem.at[k, g], recv, peer)
        copy.start()
        started.append(copy)

    def whole(ref, sem):
        pltpu.make_async_copy(ref, ref, sem).wait()

    spans = [pl.ds(first, count) for _, first, count in GROUPS]

    def along_z(source, landing, send, g):
        pltpu.make_async_copy(source(spot), landing, z_recv.at[g]).start()

        def spread(d):
            i = other_spot(d)
            remote(source(i), landing, send, z_recv.at[g], column(i)).start()

        def both_ways(k, carry):
            spread(k)
            spread(COLUMN - k)
            return carry

        lax.fori_loop(1, COLUMN // 2, both_ways, 0)
        spread(COLUMN // 2)

    every = slice(None)
    early = 0
    for g, bins in enumerate(spans):
        if GROUPS[g][0] == "p":
            early += GROUPS[g][2]
            block = s_ref.at[:, :, bins]
            start(6, g, block, p_ref.at[x, :, :, bins], x_recv.at[0, g], to_right)
            start(7, g, block, p_ref.at[x, :, :, bins], x_recv.at[1, g], to_left)
            pltpu.make_async_copy(block, p_ref.at[x, :, :, bins], p_sem.at[0, g]).start()
    for g, bins in enumerate(spans):
        if GROUPS[g][0] != "p":
            along_z(lambda i: s_ref.at[:, i, bins], t_ref.at[x, :, bins, spot], z_send, g)

    def part(chan_y, xs, bins, lo):
        return r_ref.at[chan_y, xs, bins, pl.ds(lo * COLUMN, COLUMN)]

    def along_y(g, bins, xs):
        landing = part(y_hi, xs, bins, y_lo)
        other, own = t_ref.at[xs, 1 - y_lo, bins], t_ref.at[xs, y_lo, bins]
        start(0, g, other, landing, y_recv.at[0, g], to_up)
        start(1, g, other, landing, y_recv.at[1, g], to_down)
        start(2, g, own, landing, y_recv.at[2, g], at_y(2))
        pltpu.make_async_copy(own, landing, own_sem.at[g]).start()

    def wait_y(g, bins, xs):
        for k, step in ((0, 3), (1, 1), (2, 2)):
            other = (y + step) % Y_SIZE
            whole(part(other // 2, xs, bins, other % 2), y_recv.at[k, g])
        whole(part(y_hi, xs, bins, y_lo), own_sem.at[g])

    def act(what, g):
        bins = spans[g]
        if what == "zy":
            whole(t_ref.at[x, :, bins], z_recv.at[g])
            along_y(g, bins, x)
        elif what == "yx":
            wait_y(g, bins, x)
            block = r_ref.at[:, x, bins]
            start(6, g, block, block, x_recv.at[0, g], to_right)
            start(7, g, block, block, x_recv.at[1, g], to_left)
        elif what == "x2y":
            whole(r_ref.at[:, left, bins], x_recv.at[0, g])
            block = r_ref.at[0, left, bins]
            start(8, g, block, block, x_recv.at[2, g], to_right)
            whole(r_ref.at[:, right, bins], x_recv.at[1, g])
            block = r_ref.at[1, right, bins]
            start(9, g, block, block, x_recv.at[3, g], to_left)
        elif what == "ey":
            for k in range(2):
                whole(r_ref.at[k, far, bins], x_recv.at[2 + k, g])
        elif what == "zx":
            block = t_ref.at[x, :, bins]
            whole(block, z_recv.at[g])
            start(6, g, block, block, x_recv.at[0, g], to_right)
            start(7, g, block, block, x_recv.at[1, g], to_left)
        elif what == "x2x":
            whole(t_ref.at[left, :, bins], x_recv.at[0, g])
            block = t_ref.at[left, 0, bins]
            start(8, g, block, block, x_recv.at[2, g], to_right)
            whole(t_ref.at[right, :, bins], x_recv.at[1, g])
            block = t_ref.at[right, 1, bins]
            start(9, g, block, block, x_recv.at[3, g], to_left)
        elif what == "x2p":
            whole(p_ref.at[left, :, :, bins], x_recv.at[0, g])
            block = p_ref.at[left, 0, :, bins]
            start(8, g, block, block, x_recv.at[2, g], to_right)
            whole(p_ref.at[right, :, :, bins], x_recv.at[1, g])
            block = p_ref.at[right, 1, :, bins]
            start(9, g, block, block, x_recv.at[3, g], to_left)
        elif what == "zp":
            whole(p_ref.at[x, :, :, bins], p_sem.at[0, g])
            for k in range(2):
                whole(p_ref.at[far, k, :, bins], x_recv.at[2 + k, g])
            along_z(lambda i: p_ref.at[:, :, i, bins], t_ref.at[:, :, bins, spot], p_sem.at[1, g], g)
        elif what == "y1":
            if GROUPS[g][0] == "p":
                whole(t_ref.at[:, :, bins], z_recv.at[g])
            else:
                for k in range(2):
                    whole(t_ref.at[far, k, bins], x_recv.at[2 + k, g])
            along_y(g, bins, every)
        elif what == "ex":
            wait_y(g, bins, every)

    for what, g in ORDER:
        act(what, g)
    whole(s_ref.at[:, pl.ds(0, COLUMN - 1), pl.ds(0, BINS - early)], z_send)
    for g, bins in enumerate(spans):
        if GROUPS[g][0] == "p":
            whole(p_ref.at[:, :, pl.ds(0, COLUMN - 1), bins], p_sem.at[1, g])
    for copy in started:
        copy.wait_send()


def gathered_spectra(raw, offsets, quality):
    n = len(GROUPS)
    inputs = [pltpu.with_memory_space_constraint(a, pltpu.HBM) for a in (offsets, quality, jnp.asarray(table_seeds()), raw)]
    return pl.pallas_call(
        gather_kernel,
        out_shape=jax.ShapeDtypeStruct((2, X_SIZE, BINS, WIN, 8, LANES), jnp.bfloat16),
        in_specs=[pl.BlockSpec(memory_space=pltpu.HBM)] * 4,
        out_specs=pl.BlockSpec(memory_space=pltpu.VMEM),
        scratch_shapes=[
            pltpu.VMEM((2, COLUMN, BINS, 8, LANES), jnp.bfloat16),
            pltpu.VMEM((X_SIZE, 2, BINS, COLUMN, 8, LANES), jnp.bfloat16),
            pltpu.VMEM((X_SIZE, 2, COLUMN, BINS, 8, LANES), jnp.bfloat16),
            pltpu.SemaphoreType.DMA,
            pltpu.SemaphoreType.DMA((10, n)),
            pltpu.SemaphoreType.DMA((n,)),
            pltpu.SemaphoreType.DMA((3, n)),
            pltpu.SemaphoreType.DMA((4, n)),
            pltpu.SemaphoreType.DMA((2, n)),
            pltpu.SemaphoreType.DMA((n,)),
            pltpu.SMEM((LOCAL_W,), jnp.int32),
            pltpu.VMEM((LOCAL_W, LANES), jnp.int32),
            pltpu.VMEM((4, F, LANES), jnp.float32),
            pltpu.VMEM((2 * F, L), jnp.bfloat16),
            pltpu.VMEM((LOCAL_W, SEG, LANES), jnp.bfloat16),
            pltpu.VMEM((2, SEG, LANES), jnp.float32),
            pltpu.VMEM((2, L, 2 * LANES), jnp.bfloat16),
            pltpu.VMEM((2 * F, 2 * LANES), jnp.float32),
            pltpu.VMEM((F * 8, LANES), jnp.float32),
            pltpu.SemaphoreType.DMA((LOCAL_W + 3,)),
        ],
        compiler_params=pltpu.CompilerParams(
            collective_id=0, has_side_effects=True, vmem_limit_bytes=40 << 20),
        name="gather",
    )(*inputs)


def stack_kernel(r_ref, out_hbm, out_ref, out_sem):
    chan = lax.axis_index("chan")
    row = lax.broadcasted_iota(jnp.int32, (WIN, 8, LANES), 1)
    scale = 1.0 / math.sqrt(WINDOWS)

    def one_bin(f, carry):
        own = r_ref[chan, f].astype(jnp.float32)
        turned = pltpu.roll(own.reshape(WIN, 8, LANES), 4, 1)
        turned = jnp.where(row < 4, turned, -turned).reshape(WIN * 8, LANES)
        ours = jnp.concatenate([own.T, turned.T], 0).astype(jnp.bfloat16)
        for k in range(0, CHAN, 2):
            pair = jnp.concatenate([r_ref[k, f], r_ref[k + 1, f]], 1)
            both = jnp.dot(ours, pair, preferred_element_type=jnp.float32) * scale
            lanes = slice(k * LANES, (k + 2) * LANES)
            out_ref[f, 0, :, lanes] = both[:LANES].astype(jnp.bfloat16)
            out_ref[f, 1, :, lanes] = both[LANES:].astype(jnp.bfloat16)
        pltpu.make_async_copy(out_ref.at[f], out_hbm.at[f], out_sem.at[f]).start()
        return carry

    lax.fori_loop(0, BINS, one_bin, 0, unroll=6)
    for f in range(BINS):
        pltpu.make_async_copy(out_ref.at[f], out_hbm.at[f], out_sem.at[f]).wait()


def stacked(r):
    return pl.pallas_call(
        stack_kernel,
        out_shape=jax.ShapeDtypeStruct((BINS, 2, LANES, C), jnp.bfloat16),
        in_specs=[pl.BlockSpec(memory_space=pltpu.VMEM)],
        out_specs=pl.BlockSpec(memory_space=pl.ANY),
        scratch_shapes=[
            pltpu.VMEM((BINS, 2, LANES, C), jnp.bfloat16),
            pltpu.SemaphoreType.DMA((BINS,)),
        ],
        compiler_params=pltpu.CompilerParams(vmem_limit_bytes=24 << 20),
        name="stack",
    )(r)


def local(raw, offsets, quality):
    r = gathered_spectra(raw, offsets, quality)
    return stacked(r.reshape(CHAN, BINS, WIN * 8, LANES))


def solution(mesh):
    in_specs = (P("win", None, "chan"), P("win"), P("win", "chan"))
    out_specs = P("win", None, "chan", None)
    return jax.shard_map(local, mesh=mesh, in_specs=in_specs, out_specs=out_specs, check_vma=False)
```
